128 devices in a mesh: row: 8 (over y_hi, z), col: 16 (over y_lo, x, core).
Axes of the slice: x: 4, y: 4 (y_hi: 2, y_lo: 2; y = y_hi * 2 + y_lo), z: 4, core: 2. Of those that a mesh axis runs over, the one named last changes fastest.
Arguments:
- covariance: float32 [16384, 16384], P('row', 'col'), may hold values from -6 to 6
- wind_direction: int32 [2, 16384], replicated, may hold values from 0 to 3
- wind_speed: int32 [2, 16384], replicated, may hold values from 0 to 7
- speed_table: float32 [2, 8], replicated, may hold values from 0.05 to 0.4
- diffusivity: float32 [128], replicated, may hold values from 0.005 to 0.05
Outputs:
- predicted_covariance: float32 [16384, 16384], P('row', 'col')
The draws below stay inside these ranges and needn't reach their ends.
All inputs are finite; a program needn't handle non-finite values.
Results may differ from the reference program's by a relative error of at most 0.00002.
Values sent between devices are 32-bit elements; how exact they have to be, the bound alone decides.
A program may use at most 192 MiB of HBM per device.

```python
import math
import jax
import jax.numpy as jnp
from jax import lax

NLAT = 128
NLON = 128
SUBSTEPS = 2
CLASSES = 8
MESH_POINT_COUNT = 16384


def touch_ends(entries, key, low, largest):
    shape = entries.shape
    spot = [jax.random.randint(jax.random.fold_in(key, axis), (), 0, shape[axis]) for axis in range(len(shape))]
    entries = entries.at[tuple(spot)].set(low)
    longest = shape.index(max(shape))
    spot[longest] = (spot[longest] + 1) % shape[longest]
    return entries.at[tuple(spot)].set(largest)


def block_scale(stream_key, extent, cuts, least, largest):
    gain, own = 1.0, jax.random.fold_in(stream_key, 6)
    for axis_at, blocks in cuts:
        heights = jnp.exp(jax.random.uniform(jax.random.fold_in(own, axis_at), (blocks,), jnp.float32, least / len(cuts), largest / len(cuts)))
        gain = gain * jnp.repeat(heights, extent[axis_at] // blocks).reshape([-1 if axis == axis_at else 1 for axis in range(len(extent))])
    return gain


def bell_draw(key, shape, deviation, reach, split=(), kind=jnp.bfloat16):
    values = jax.random.normal(key, shape, jnp.float32) * deviation
    if len(split) > 0:
        values = block_scale(key, shape, split, -0.22, 0.18) * values
    return jnp.clip(values, min=-reach, max=reach).astype(kind)


def setup_inputs(seed: int = 0) -> dict:
    key_list = jax.random.split(jax.random.key(seed), 6)
    covariance = bell_draw(key_list[0], (MESH_POINT_COUNT, MESH_POINT_COUNT), 1.0, 6.0, ((0, 8), (1, 16)), jnp.float32)
    wind_direction = touch_ends(jax.random.randint(key_list[1], (SUBSTEPS, MESH_POINT_COUNT), 0, 4), jax.random.fold_in(key_list[1], 1), 0, 3).astype(jnp.int32)
    wind_speed = touch_ends(jax.random.randint(key_list[2], (SUBSTEPS, MESH_POINT_COUNT), 0, CLASSES), jax.random.fold_in(key_list[2], 1), 0, CLASSES - 1).astype(jnp.int32)
    speed_table = jnp.clip(jax.random.uniform(key_list[3], (2, CLASSES), jnp.float32, 0.05, 0.4), 0.05, 0.4)
    diffusivity = jnp.clip(jnp.exp(jax.random.uniform(key_list[4], (NLAT,), jnp.float32, math.log(0.005), math.log(0.05))), 0.005, 0.05)
    return dict(covariance=covariance, wind_direction=wind_direction, wind_speed=wind_speed, speed_table=speed_table, diffusivity=diffusivity)


def build_coefficients(wind_direction, wind_speed, speed_table, diffusivity, nlat, nlon):
    substeps = wind_direction.shape[0]
    category_list = speed_table.shape[1]
    onehot = (wind_speed[:, :, None] == jnp.arange(category_list, dtype=jnp.int32)).astype(speed_table.dtype)
    lon_courant = jnp.sum(onehot * speed_table[0], axis=2).reshape(substeps, nlat, nlon)
    lat_courant = jnp.sum(onehot * speed_table[1], axis=2).reshape(substeps, nlat, nlon)
    eastward = (wind_direction % 2 == 0).astype(speed_table.dtype).reshape(substeps, nlat, nlon)
    northward = (wind_direction // 2 == 0).astype(speed_table.dtype).reshape(substeps, nlat, nlon)
    diffusion = diffusivity[None, :, None]
    center = 1.0 - lon_courant - lat_courant - 4.0 * diffusion
    western = lon_courant * eastward + diffusion
    eastern = lon_courant * (1.0 - eastward) + diffusion
    southern = lat_courant * northward + diffusion
    northern = lat_courant * (1.0 - northward) + diffusion
    return jnp.stack([center, western, eastern, southern, northern], axis=1)


def substep(tracer, weights):
    padded = jnp.pad(tracer, ((1, 1), (0, 0), (0, 0)))
    southern = padded[:-2]
    northern = padded[2:]
    return (weights[0] * tracer + weights[1] * jnp.roll(tracer, 1, axis=1)
            + weights[2] * jnp.roll(tracer, -1, axis=1) + weights[3] * southern + weights[4] * northern)


def apply_operator(tracer, weight_table):
    for section_idx in range(weight_table.shape[0]):
        tracer = substep(tracer, weight_table[section_idx])
    return tracer


def reference(covariance, wind_direction, wind_speed, speed_table, diffusivity):
    weight_table = build_coefficients(wind_direction, wind_speed, speed_table, diffusivity, NLAT, NLON)[..., None]
    col_width = MESH_POINT_COUNT // 16

    def first_pass(panel_number):
        column_block = lax.dynamic_slice_in_dim(covariance, panel_number * col_width, col_width, 1)
        moved_block = apply_operator(column_block.reshape(NLAT, NLON, col_width), weight_table)
        return moved_block.reshape(MESH_POINT_COUNT, col_width)

    advected = lax.map(first_pass, jnp.arange(16, dtype=jnp.int32))
    advected = jnp.transpose(advected, (1, 0, 2)).reshape(MESH_POINT_COUNT, MESH_POINT_COUNT)

    def second_pass_rims(panel_number):
        row_block = lax.dynamic_slice_in_dim(advected, panel_number * col_width, col_width, 0)
        moved_block = apply_operator(row_block.T.reshape(NLAT, NLON, col_width), weight_table)
        return moved_block.reshape(MESH_POINT_COUNT, col_width).T

    predicted_covariance = lax.map(second_pass_rims, jnp.arange(16, dtype=jnp.int32))
    return predicted_covariance.reshape(MESH_POINT_COUNT, MESH_POINT_COUNT)
```

```python
import functools

import jax
import jax.numpy as jnp
from jax import lax
from jax.experimental import pallas as pl
from jax.experimental.pallas import tpu as pltpu
from jax.sharding import PartitionSpec as P

NLAT = 128
NLON = 128
CLASSES = 8
MESH = pl.DeviceIdType.MESH
HALO = 2 * NLON

X_CHUNKS = ((0, 2), (14, 2), (2, 4), (6, 4), (10, 2), (12, 2))
COL_ROWS = 32
ROW_BLOCK = 32


def lookup(codes, tab_ref, line):
    value = jnp.full(codes.shape, tab_ref[line, 0], jnp.float32)
    for cls in range(1, CLASSES):
        value = jnp.where(codes == cls, tab_ref[line, cls], value)
    return value


def weights_of(lat, wd_ref, ws_ref, tab_ref, dif_ref):
    inside = jnp.logical_and(lat >= 0, lat < NLAT)
    lat = jnp.clip(lat, 0, NLAT - 1)
    spot = pl.ds(pl.multiple_of(lat * NLON, NLON), NLON)
    direction = wd_ref[:, spot]
    speed = ws_ref[:, spot]
    u = lookup(speed, tab_ref, 0)
    v = lookup(speed, tab_ref, 1)
    e = jnp.where((direction & 1) == 0, 1.0, 0.0)
    n = jnp.where(direction < 2, 1.0, 0.0)
    k = dif_ref[lat]
    keep = jnp.where(inside, 1.0, 0.0)
    return [
        w * keep
        for w in (
            1.0 - u - v - 4.0 * k,
            u * e + k,
            u * (1.0 - e) + k,
            v * n + k,
            v * (1.0 - n) + k,
        )
    ]


def kernel(
    n_rows, n_cols, lat_r, lat_c,
    cov, wd_ref, ws_ref, tab_ref, dif_ref, out,
    X, B, CW, RW, G, lsem, xs, xr, zs, zr,
):
    r = lax.axis_index("row")
    c = lax.axis_index("col")
    left, right, up, down = c > 0, c < n_cols - 1, r > 0, r < n_rows - 1
    rows, cols = lat_r * NLON, lat_c * NLON
    at_left, at_right = {"row": r, "col": c - 1}, {"row": r, "col": c + 1}
    at_up, at_down = {"row": r - 1, "col": c}, {"row": r + 1, "col": c}

    own = [(0, HALO), (rows - HALO, HALO), (HALO, rows - 2 * HALO)]

    def own_copy(i):
        start, size = own[i]
        return pltpu.make_async_copy(
            cov.at[pl.ds(start, size), :], X.at[pl.ds(start, size), pl.ds(HALO, cols)], lsem.at[i]
        )

    barrier = pltpu.get_barrier_semaphore()
    sides = ((left, at_left), (right, at_right), (up, at_up), (down, at_down))
    for have, where in sides:
        @pl.when(have)
        def _():
            pl.semaphore_signal(barrier, inc=1, device_id=where, device_id_type=MESH)
    for i in range(3):
        own_copy(i).start()
    pl.semaphore_wait(barrier, sum(jnp.where(have, 1, 0) for have, _ in sides))

    def x_copy(i, side):
        lat, count = X_CHUNKS[i]
        span = pl.ds(lat * NLON, count * NLON)
        if side == 0:
            src, dst, where = cov.at[span, pl.ds(cols - HALO, HALO)], X.at[span, pl.ds(0, HALO)], at_right
        else:
            src, dst, where = cov.at[span, pl.ds(0, HALO)], X.at[span, pl.ds(HALO + cols, HALO)], at_left
        return pltpu.make_async_remote_copy(
            src_ref=src, dst_ref=dst, send_sem=xs.at[side, i], recv_sem=xr.at[side, i],
            device_id=where, device_id_type=MESH,
        )

    for i in range(len(X_CHUNKS)):
        @pl.when(right)
        def _():
            x_copy(i, 0).start()

        @pl.when(left)
        def _():
            x_copy(i, 1).start()

    Z_PIECES = ((2, 2), (4, 2), (0, 2), (6, 2))

    def z_copy(i, side):
        lat, count = Z_PIECES[i]
        span = pl.ds(lat * NLON, count * NLON)
        if side == 0:
            src, dst, where = B.at[pl.ds(rows, HALO), span], B.at[pl.ds(0, HALO), span], at_down
        else:
            src, dst, where = B.at[pl.ds(HALO, HALO), span], B.at[pl.ds(HALO + rows, HALO), span], at_up
        return pltpu.make_async_remote_copy(
            src_ref=src, dst_ref=dst, send_sem=zs.at[side, i], recv_sem=zr.at[side, i],
            device_id=where, device_id_type=MESH,
        )

    def z_start(i, side):
        @pl.when(down if side == 0 else up)
        def _():
            z_copy(i, side).start()

    def z_wait(i, side):
        @pl.when(up if side == 0 else down)
        def _():
            z_copy(i, side).wait_recv()

    def x_wait(i):
        @pl.when(left)
        def _():
            x_copy(i, 0).wait_recv()

        @pl.when(right)
        def _():
            x_copy(i, 1).wait_recv()

    @pl.when(jnp.logical_not(left))
    def _():
        X[:, pl.ds(0, HALO)] = jnp.zeros((rows, HALO), jnp.float32)

    @pl.when(jnp.logical_not(right))
    def _():
        X[:, pl.ds(HALO + cols, HALO)] = jnp.zeros((rows, HALO), jnp.float32)

    @pl.when(jnp.logical_not(up))
    def _():
        B[pl.ds(0, HALO), :] = jnp.zeros((HALO, cols), jnp.float32)

    @pl.when(jnp.logical_not(down))
    def _():
        B[pl.ds(HALO + rows, HALO), :] = jnp.zeros((HALO, cols), jnp.float32)

    def col_table(i, carry):
        for k, w in enumerate(weights_of(c * lat_c + i - 1, wd_ref, ws_ref, tab_ref, dif_ref)):
            for s in range(2):
                CW[s * 5 + k, i] = jnp.broadcast_to(w[s : s + 1], (8, NLON))
        return carry

    lax.fori_loop(0, lat_c + 2, col_table, 0)

    def stencil(f, west, east, south, north, w):
        return w[0] * f + w[1] * west + w[2] * east + w[3] * south + w[4] * north

    def column_operator(start, count, lo, hi):
        tiles = COL_ROWS // 8

        def lane_step(field, l, s):
            f = field[l]
            w = [CW[s * 5 + k, l + 1][None] for k in range(5)]
            return stencil(f, pltpu.roll(f, 1, 2), pltpu.roll(f, NLON - 1, 2), field[l - 1], field[l + 1], w)

        def body(i, carry):
            at = pl.multiple_of(start + i * COL_ROWS, COL_ROWS)
            f, g = {}, {}

            def fetch(l):
                f[l] = X[pl.ds(at, COL_ROWS), pl.ds(HALO + l * NLON, NLON)].reshape(tiles, 8, NLON)

            fetch(lo - 2)
            fetch(lo - 1)
            for l in range(lo - 1, hi + 1):
                fetch(l + 1)
                g[l] = lane_step(f, l, 0)
                if l - 1 >= lo:
                    o = lane_step(g, l - 1, 1)
                    B[pl.ds(HALO + at, COL_ROWS), pl.ds((l - 1) * NLON, NLON)] = o.reshape(COL_ROWS, NLON)
            return carry

        lax.fori_loop(0, count // COL_ROWS, body, 0)

    def row_step(src, base, span, s, lat, store):
        above, below = base - NLON, base + NLON
        for b in range(NLON // ROW_BLOCK):
            o = b * ROW_BLOCK
            prev, nxt = (o - 8) % NLON, (o + ROW_BLOCK) % NLON
            f = src[pl.ds(base + o, ROW_BLOCK), span]
            wide = jnp.concatenate([src[pl.ds(base + prev, 8), span], f, src[pl.ds(base + nxt, 8), span]], axis=0)
            west = pltpu.roll(wide, 1, 0)[8 : 8 + ROW_BLOCK]
            east = pltpu.roll(wide, ROW_BLOCK + 15, 0)[8 : 8 + ROW_BLOCK]
            w = []
            for k in range(5):
                t = RW[s * 5 + k, lat + 1, pl.ds(o, ROW_BLOCK), :]
                w.append(jnp.concatenate([t, t], axis=1))
            south = src[pl.ds(above + o, ROW_BLOCK), span]
            north = src[pl.ds(below + o, ROW_BLOCK), span]
            store(o, stencil(f, west, east, south, north, w))

    def row_operator(lat0, count, pairs):
        first, n, stride = pairs

        def pair(p, carry):
            span = pl.ds(pl.multiple_of((first + p * stride) * HALO, HALO), HALO)

            def one(i, inner):
                lat = lat0 - 1 + i

                def store(o, value):
                    G[pl.ds(pl.multiple_of(i * NLON, NLON) + o, ROW_BLOCK), :] = value

                row_step(B, pl.multiple_of(HALO + lat * NLON, NLON), span, 0, lat, store)
                return inner

            lax.fori_loop(0, count + 2, one, 0)

            def two(i, inner):
                lat = lat0 + i

                def store(o, value):
                    out[pl.ds(pl.multiple_of(lat * NLON, NLON) + o, ROW_BLOCK), span] = value

                row_step(G, pl.multiple_of((i + 1) * NLON, NLON), slice(None), 1, lat, store)
                return inner

            lax.fori_loop(0, count, two, 0)
            return carry

        lax.fori_loop(0, n, pair, 0)

    INNER, OUTER = (1, 2, 1), (0, 2, 3)
    last = lat_c - 2

    own_copy(1).wait()
    column_operator(rows - HALO, HALO, 2, last)
    for i in range(2):
        z_start(i, 0)
    own_copy(0).wait()
    column_operator(0, HALO, 2, last)
    for i in range(2):
        z_start(i, 1)

    own_copy(2).wait()
    column_operator(HALO, rows - 2 * HALO, 2, last)

    def row_table(i, carry):
        lines = []
        ws = weights_of(r * lat_r + i - 1, wd_ref, ws_ref, tab_ref, dif_ref)
        for s in range(2):
            lines += [w[s : s + 1] for w in ws]
        block = jnp.concatenate(lines + [jnp.zeros((6, NLON), jnp.float32)], axis=0)
        turned = block.T
        for q in range(10):
            RW[q, i] = jnp.broadcast_to(turned[:, q : q + 1], (NLON, NLON))
        return carry

    lax.fori_loop(0, lat_r + 2, row_table, 0)

    def edges(i):
        lat, count = X_CHUNKS[i]
        x_wait(i)
        column_operator(lat * NLON, count * NLON, 0, 2)
        column_operator(lat * NLON, count * NLON, last, lat_c)

    edges(1)
    for i in (2, 3):
        z_start(i, 0)
    edges(0)
    for i in (2, 3):
        z_start(i, 1)

    row_operator(2, lat_r - 4, INNER)
    edges(2)
    row_operator(2, 2, OUTER)
    for i in (0, 1):
        z_wait(i, 0)
        z_wait(i, 1)
    row_operator(0, 2, INNER)
    row_operator(lat_r - 2, 2, INNER)
    edges(3)
    row_operator(4, 4, OUTER)
    edges(4)
    row_operator(8, 2, OUTER)
    edges(5)
    row_operator(10, 4, OUTER)
    for i in (2, 3):
        z_wait(i, 0)
        z_wait(i, 1)
    row_operator(0, 2, OUTER)
    row_operator(lat_r - 2, 2, OUTER)

    for i in range(len(X_CHUNKS)):
        @pl.when(right)
        def _():
            x_copy(i, 0).wait_send()

        @pl.when(left)
        def _():
            x_copy(i, 1).wait_send()
    for i in range(len(Z_PIECES)):
        @pl.when(down)
        def _():
            z_copy(i, 0).wait_send()

        @pl.when(up)
        def _():
            z_copy(i, 1).wait_send()


def solution(mesh):
    n_rows, n_cols = mesh.shape["row"], mesh.shape["col"]
    lat_r, lat_c = NLAT // n_rows, NLAT // n_cols

    def local(cov, wd, ws, tab, dif):
        rows, cols = cov.shape
        vmem = pl.BlockSpec(memory_space=pltpu.VMEM)
        smem = pl.BlockSpec(memory_space=pltpu.SMEM)
        f32 = jnp.float32
        return pl.pallas_call(
            functools.partial(kernel, n_rows, n_cols, lat_r, lat_c),
            out_shape=pltpu.VMEM((rows, cols), f32),
            in_specs=[pl.BlockSpec(memory_space=pl.ANY), vmem, vmem, smem, smem],
            out_specs=vmem,
            scratch_shapes=[
                pltpu.VMEM((rows, cols + 2 * HALO), f32),
                pltpu.VMEM((rows + 2 * HALO, cols), f32),
                pltpu.VMEM((10, lat_c + 2, 8, NLON), f32),
                pltpu.VMEM((10, lat_r + 2, NLON, NLON), f32),
                pltpu.VMEM(((lat_r - 2) * NLON, HALO), f32),
                pltpu.SemaphoreType.DMA((3,)),
                pltpu.SemaphoreType.DMA((2, len(X_CHUNKS))),
                pltpu.SemaphoreType.DMA((2, len(X_CHUNKS))),
                pltpu.SemaphoreType.DMA((2, 4)),
                pltpu.SemaphoreType.DMA((2, 4)),
            ],
            compiler_params=pltpu.CompilerParams(
                collective_id=0, has_side_effects=True, vmem_limit_bytes=50 << 20
            ),
        )(cov, wd, ws, tab, dif)

    return jax.shard_map(
        local,
        mesh=mesh,
        in_specs=(P("row", "col"), P(), P(), P(), P()),
        out_specs=P("row", "col"),
        check_vma=False,
    )
```

```python
import functools

import jax
import jax.numpy as jnp
from jax import lax
from jax.experimental import pallas as pl
from jax.experimental.pallas import tpu as pltpu
from jax.sharding import PartitionSpec as P

NLAT = 128
NLON = 128
CLASSES = 8
MESH = pl.DeviceIdType.MESH
HALO = 2 * NLON
PAD = 8

X_CHUNKS = ((14, 2), (0, 2), (2, 4), (6, 4), (10, 2), (12, 2))
X_RELAYED = (2, 3)
Z_PIECES = ((2, 2), (4, 2), (0, 2), (6, 2))
Z_RELAYED = (1, 3)
ROW_BLOCK = 32


def lookup(codes, tab_ref, line):
    value = jnp.full(codes.shape, tab_ref[line, 0], jnp.float32)
    for cls in range(1, CLASSES):
        value = jnp.where(codes == cls, tab_ref[line, cls], value)
    return value


def weights_of(lat, wd_ref, ws_ref, tab_ref, dif_ref):
    inside = jnp.logical_and(lat >= 0, lat < NLAT)
    lat = jnp.clip(lat, 0, NLAT - 1)
    spot = pl.ds(pl.multiple_of(lat * NLON, NLON), NLON)
    direction = wd_ref[:, spot]
    speed = ws_ref[:, spot]
    u = lookup(speed, tab_ref, 0)
    v = lookup(speed, tab_ref, 1)
    e = jnp.where((direction & 1) == 0, 1.0, 0.0)
    n = jnp.where(direction < 2, 1.0, 0.0)
    k = dif_ref[lat]
    keep = jnp.where(inside, 1.0, 0.0)
    return [
        w * keep
        for w in (
            1.0 - u - v - 4.0 * k,
            u * e + k,
            u * (1.0 - e) + k,
            v * n + k,
            v * (1.0 - n) + k,
        )
    ]


def kernel(
    n_rows, n_cols, lat_r, lat_c,
    cov, wd_ref, ws_ref, tab_ref, dif_ref, out,
    X, B, CW, RW, G, RX, RZ,
    lsem, xs, xr, zs, zr, rxs, rxr, rzs, rzr,
):
    r = lax.axis_index("row")
    c = lax.axis_index("col")
    left, right, up, down = c > 0, c < n_cols - 1, r > 0, r < n_rows - 1
    rows, cols = lat_r * NLON, lat_c * NLON

    def at(row, col):
        return {"row": row, "col": col}

    mid_r, mid_c = n_rows // 2, n_cols // 2
    q = lax.rem(c, mid_c)
    z_cross = jnp.logical_or(q < 2, q >= mid_c - 2)
    p = lax.rem(r, mid_r)
    x_cross = jnp.logical_or(p == 0, p == mid_r - 1)

    def z_role(row):
        return jnp.logical_and(z_cross, r == row)

    def x_role(col):
        return jnp.logical_and(x_cross, c == col)

    end_r, end_c = n_rows - 1, n_cols - 1
    peers = [(left, at(r, c - 1)), (right, at(r, c + 1)), (up, at(r - 1, c)), (down, at(r + 1, c))]
    for a, b in ((mid_r - 1, 0), (0, mid_r), (mid_r, end_r), (end_r, mid_r - 1)):
        peers += [(z_role(a), at(b, c)), (z_role(b), at(a, c))]
    for a, b in ((mid_c - 1, end_c), (end_c, mid_c), (mid_c, 0), (0, mid_c - 1)):
        peers += [(x_role(a), at(r, b)), (x_role(b), at(r, a))]

    own = [(rows - HALO, HALO), (0, HALO), (HALO, rows - 2 * HALO)]

    def own_copy(i):
        start, size = own[i]
        return pltpu.make_async_copy(
            cov.at[pl.ds(start, size), :], X.at[pl.ds(start, size), pl.ds(HALO, cols)], lsem.at[i]
        )

    barrier = pltpu.get_barrier_semaphore()
    for have, where in peers:
        @pl.when(have)
        def _():
            pl.semaphore_signal(barrier, inc=1, device_id=where, device_id_type=MESH)
    for i in range(3):
        own_copy(i).start()

    def col_table(i, carry):
        for k, w in enumerate(weights_of(c * lat_c + i - 1, wd_ref, ws_ref, tab_ref, dif_ref)):
            for s in range(2):
                CW[s * 5 + k, i] = jnp.broadcast_to(w[s : s + 1], (8, NLON))
        return carry

    lax.fori_loop(0, lat_c + 2, col_table, 0)

    pl.semaphore_wait(barrier, sum(jnp.where(have, 1, 0) for have, _ in peers))

    def remote(src, dst, send, recv, where):
        return lambda: pltpu.make_async_remote_copy(
            src_ref=src, dst_ref=dst, send_sem=send, recv_sem=recv, device_id=where, device_id_type=MESH
        )

    def x_halo(i, side):
        lat, count = X_CHUNKS[i]
        return X.at[pl.ds(lat * NLON, count * NLON), pl.ds(0 if side == 0 else HALO + cols, HALO)]

    def x_copies(i, side):
        lat, count = X_CHUNKS[i]
        src = cov.at[pl.ds(lat * NLON, count * NLON), pl.ds(cols - HALO if side == 0 else 0, HALO)]
        have, where = (right, at(r, c + 1)) if side == 0 else (left, at(r, c - 1))
        direct = remote(src, x_halo(i, side), xs.at[side, i], xr.at[side, i], where)
        if i not in X_RELAYED:
            return [(have, direct)]
        slot = X_RELAYED.index(i)
        source, relay = (mid_c - 1, end_c) if side == 0 else (mid_c, 0)
        by_relay = remote(src, RX.at[slot], xs.at[side, i], rxr.at[slot], at(r, relay))
        here = x_role(source)
        return [(jnp.logical_and(have, jnp.logical_not(here)), direct), (here, by_relay)]

    def x_forwards(slot):
        i = X_RELAYED[slot]
        return [
            (x_role(end_c), remote(RX.at[slot], x_halo(i, 0), rxs.at[slot], xr.at[0, i], at(r, mid_c))),
            (x_role(0), remote(RX.at[slot], x_halo(i, 1), rxs.at[slot], xr.at[1, i], at(r, mid_c - 1))),
        ]

    def z_halo(i, side):
        lat, count = Z_PIECES[i]
        return B.at[pl.ds(lat, count), pl.ds(0 if side == 0 else lat_r + 2, 2), pl.ds(PAD, NLON), :]

    def z_copies(i, side):
        lat, count = Z_PIECES[i]
        src = B.at[pl.ds(lat, count), pl.ds(lat_r if side == 0 else 2, 2), pl.ds(PAD, NLON), :]
        have, where = (down, at(r + 1, c)) if side == 0 else (up, at(r - 1, c))
        direct = remote(src, z_halo(i, side), zs.at[side, i], zr.at[side, i], where)
        if i not in Z_RELAYED:
            return [(have, direct)]
        slot = Z_RELAYED.index(i)
        source, relay = (mid_r - 1, 0) if side == 0 else (mid_r, end_r)
        by_relay = remote(src, RZ.at[slot], zs.at[side, i], rzr.at[slot], at(relay, c))
        here = z_role(source)
        return [(jnp.logical_and(have, jnp.logical_not(here)), direct), (here, by_relay)]

    def z_forwards(slot):
        i = Z_RELAYED[slot]
        return [
            (z_role(0), remote(RZ.at[slot], z_halo(i, 0), rzs.at[slot], zr.at[0, i], at(mid_r, c))),
            (z_role(end_r), remote(RZ.at[slot], z_halo(i, 1), rzs.at[slot], zr.at[1, i], at(mid_r - 1, c))),
        ]

    def start(copies):
        for have, copy in copies:
            @pl.when(have)
            def _():
                copy().start()

    def wait_sent(copies):
        for have, copy in copies:
            @pl.when(have)
            def _():
                copy().wait_send()

    def x_forward(slot):
        @pl.when(jnp.logical_or(x_role(0), x_role(end_c)))
        def _():
            x_copies(X_RELAYED[slot], 0)[1][1]().wait_recv()

        start(x_forwards(slot))

    def z_forward(slot):
        @pl.when(jnp.logical_or(z_role(0), z_role(end_r)))
        def _():
            z_copies(Z_RELAYED[slot], 0)[1][1]().wait_recv()

        start(z_forwards(slot))

    def z_start(i, side):
        start(z_copies(i, side))

    def z_wait(i):
        lat, count = Z_PIECES[i]
        for side, have in ((0, up), (1, down)):
            @pl.when(have)
            def _():
                z_copies(i, side)[0][1]().wait_recv()

            for a in (0, 1):
                y = a + (0 if side == 0 else lat_r + 2)
                for l in range(lat, lat + count):
                    B[l, y, pl.ds(0, PAD), :] = B[l, y, pl.ds(NLON, PAD), :]
                    B[l, y, pl.ds(PAD + NLON, PAD), :] = B[l, y, pl.ds(PAD, PAD), :]

    def x_wait(i):
        for side, have in ((0, left), (1, right)):
            @pl.when(have)
            def _():
                x_copies(i, side)[0][1]().wait_recv()

    for i in range(len(X_CHUNKS)):
        for side in (0, 1):
            start(x_copies(i, side))

    def stencil(f, west, east, south, north, w):
        return w[0] * f + w[1] * west + w[2] * east + w[3] * south + w[4] * north

    tiles = NLON // 8

    def column_operator(lat0, count, spans):
        def lane_step(field, l, s):
            f = field[l]
            w = [CW[s * 5 + k, l + 1][None] for k in range(5)]
            return stencil(f, pltpu.roll(f, 1, 2), pltpu.roll(f, NLON - 1, 2), field[l - 1], field[l + 1], w)

        def body(i, carry):
            y = lat0 + i
            here = pl.ds(pl.multiple_of(y * NLON, NLON), NLON)
            for lo, hi in spans:
                f, g = {}, {}
                for l in range(lo - 2, hi + 2):
                    f[l] = X[here, pl.ds(HALO + l * NLON, NLON)].reshape(tiles, 8, NLON)
                    if l > lo - 1:
                        g[l - 1] = lane_step(f, l - 1, 0)
                    if l > lo + 1:
                        o = lane_step(g, l - 2, 1)
                        B[l - 2, y + 2, pl.ds(PAD, NLON), :] = o.reshape(NLON, NLON)
                        B[l - 2, y + 2, pl.ds(0, PAD), :] = o[tiles - 1]
                        B[l - 2, y + 2, pl.ds(PAD + NLON, PAD), :] = o[0]
            return carry

        lax.fori_loop(0, count, body, 0)

    def row_step(src, first, y, s, lat, store):
        for b in range(NLON // ROW_BLOCK):
            o = b * ROW_BLOCK
            w = [RW[s * 5 + k, lat + 1, pl.ds(o, ROW_BLOCK), :] for k in range(5)]
            for l in (0, 1):
                near = [src[first + l, y, pl.ds(PAD + o + d, ROW_BLOCK), :] for d in (0, -1, 1)]
                south = src[first + l, y - 1, pl.ds(PAD + o, ROW_BLOCK), :]
                north = src[first + l, y + 1, pl.ds(PAD + o, ROW_BLOCK), :]
                store(l, o, stencil(*near, south, north, w))

    def row_operator(lat0, count, pairs):
        first, n, stride = pairs

        def pair(j, carry):
            l0 = (first + j * stride) * 2
            span = [pl.ds(pl.multiple_of((l0 + l) * NLON, NLON), NLON) for l in (0, 1)]

            def one(i, inner):
                lat = lat0 - 1 + i

                def store(l, o, value):
                    G[l, i, pl.ds(PAD + o, ROW_BLOCK), :] = value
                    if o == 0:
                        G[l, i, pl.ds(PAD + NLON, PAD), :] = value[:PAD]
                    if o == NLON - ROW_BLOCK:
                        G[l, i, pl.ds(0, PAD), :] = value[ROW_BLOCK - PAD :]

                row_step(B, l0, lat + 2, 0, lat, store)
                return inner

            lax.fori_loop(0, count + 2, one, 0, unroll=2)

            def two(i, inner):
                lat = lat0 + i
                base = pl.multiple_of(lat * NLON, NLON)

                def store(l, o, value):
                    out[pl.ds(base + o, ROW_BLOCK), span[l]] = value

                row_step(G, 0, i + 1, 1, lat, store)
                return inner

            lax.fori_loop(0, count, two, 0, unroll=2)
            return carry

        lax.fori_loop(0, n, pair, 0)

    INNER, OUTER = (1, 2, 1), (0, 2, 3)
    inner, outer = ((2, lat_c - 2),), ((0, 2), (lat_c - 2, lat_c))

    own_copy(0).wait()
    column_operator(lat_r - 2, 2, inner)
    for i in (0, 1):
        z_start(i, 0)
    own_copy(1).wait()
    column_operator(0, 2, inner)
    for i in (0, 1):
        z_start(i, 1)

    own_copy(2).wait()
    column_operator(2, lat_r - 4, inner)

    @pl.when(jnp.logical_not(left))
    def _():
        X[:, pl.ds(0, HALO)] = jnp.zeros((rows, HALO), jnp.float32)

    @pl.when(jnp.logical_not(right))
    def _():
        X[:, pl.ds(HALO + cols, HALO)] = jnp.zeros((rows, HALO), jnp.float32)

    @pl.when(jnp.logical_not(up))
    def _():
        B[:, pl.ds(0, 2)] = jnp.zeros((lat_c, 2, NLON + 2 * PAD, NLON), jnp.float32)

    @pl.when(jnp.logical_not(down))
    def _():
        B[:, pl.ds(lat_r + 2, 2)] = jnp.zeros((lat_c, 2, NLON + 2 * PAD, NLON), jnp.float32)

    def edges(i):
        x_wait(i)
        column_operator(*X_CHUNKS[i], outer)

    edges(0)
    for i in (2, 3):
        z_start(i, 0)
    edges(1)
    for i in (2, 3):
        z_start(i, 1)
    x_forward(0)
    z_forward(0)

    def row_table(i, carry):
        lat = jnp.clip(r * lat_r + i - 1, 0, NLAT - 1)
        spot = pl.ds(pl.multiple_of(lat * NLON, NLON), NLON)
        direction, speed = wd_ref[:, spot], ws_ref[:, spot]
        u, v = lookup(speed, tab_ref, 0), lookup(speed, tab_ref, 1)
        u = jnp.where((direction & 1) == 0, u, -u)
        v = jnp.where(direction < 2, v, -v)
        k = dif_ref[lat]
        turned = jnp.concatenate([u, v, u, v], axis=0).T
        for s in range(2):
            su = jnp.broadcast_to(turned[:, s : s + 1], (NLON, NLON))
            sv = jnp.broadcast_to(turned[:, 2 + s : 3 + s], (NLON, NLON))
            RW[s * 5, i] = 1.0 - jnp.abs(su) - jnp.abs(sv) - 4.0 * k
            RW[s * 5 + 1, i] = jnp.maximum(su, 0.0) + k
            RW[s * 5 + 2, i] = jnp.maximum(-su, 0.0) + k
            RW[s * 5 + 3, i] = jnp.maximum(sv, 0.0) + k
            RW[s * 5 + 4, i] = jnp.maximum(-sv, 0.0) + k
        return carry

    lax.fori_loop(0, lat_r + 2, row_table, 0, unroll=2)

    @pl.when(jnp.logical_not(up))
    def _():
        RW[:, 0] = jnp.zeros((10, NLON, NLON), jnp.float32)

    @pl.when(jnp.logical_not(down))
    def _():
        RW[:, lat_r + 1] = jnp.zeros((10, NLON, NLON), jnp.float32)

    row_operator(2, lat_r - 4, INNER)
    edges(2)
    x_forward(1)
    row_operator(2, 2, OUTER)
    z_wait(0)
    z_wait(1)
    row_operator(0, 2, INNER)
    row_operator(lat_r - 2, 2, INNER)
    edges(3)
    row_operator(4, 4, OUTER)
    z_forward(1)
    edges(4)
    row_operator(8, 2, OUTER)
    edges(5)
    row_operator(10, 4, OUTER)
    z_wait(2)
    z_wait(3)
    row_operator(0, 2, OUTER)
    row_operator(lat_r - 2, 2, OUTER)

    for side in (0, 1):
        for i in range(len(X_CHUNKS)):
            wait_sent(x_copies(i, side))
        for i in range(len(Z_PIECES)):
            wait_sent(z_copies(i, side))
    for slot in (0, 1):
        wait_sent(x_forwards(slot))
        wait_sent(z_forwards(slot))


def solution(mesh):
    n_rows, n_cols = mesh.shape["row"], mesh.shape["col"]
    lat_r, lat_c = NLAT // n_rows, NLAT // n_cols

    def local(cov, wd, ws, tab, dif):
        rows, cols = cov.shape
        vmem = pl.BlockSpec(memory_space=pltpu.VMEM)
        smem = pl.BlockSpec(memory_space=pltpu.SMEM)
        f32 = jnp.float32
        return pl.pallas_call(
            functools.partial(kernel, n_rows, n_cols, lat_r, lat_c),
            out_shape=pltpu.VMEM((rows, cols), f32),
            in_specs=[pl.BlockSpec(memory_space=pl.ANY), vmem, vmem, smem, smem],
            out_specs=vmem,
            scratch_shapes=[
                pltpu.VMEM((rows, cols + 2 * HALO), f32),
                pltpu.VMEM((lat_c, lat_r + 4, NLON + 2 * PAD, NLON), f32),
                pltpu.VMEM((10, lat_c + 2, 8, NLON), f32),
                pltpu.VMEM((10, lat_r + 2, NLON, NLON), f32),
                pltpu.VMEM((2, lat_r - 2, NLON + 2 * PAD, NLON), f32),
                pltpu.VMEM((2, 4 * NLON, HALO), f32),
                pltpu.VMEM((2, 2, 2, NLON, NLON), f32),
                pltpu.SemaphoreType.DMA((3,)),
                pltpu.SemaphoreType.DMA((2, len(X_CHUNKS))),
                pltpu.SemaphoreType.DMA((2, len(X_CHUNKS))),
                pltpu.SemaphoreType.DMA((2, len(Z_PIECES))),
                pltpu.SemaphoreType.DMA((2, len(Z_PIECES))),
                pltpu.SemaphoreType.DMA((2,)),
                pltpu.SemaphoreType.DMA((2,)),
                pltpu.SemaphoreType.DMA((2,)),
                pltpu.SemaphoreType.DMA((2,)),
            ],
            compiler_params=pltpu.CompilerParams(
                collective_id=0, has_side_effects=True, vmem_limit_bytes=52 << 20
            ),
        )(cov, wd, ws, tab, dif)

    return jax.shard_map(
        local,
        mesh=mesh,
        in_specs=(P("row", "col"), P(), P(), P(), P()),
        out_specs=P("row", "col"),
        check_vma=False,
    )
```

```python
import functools

import jax
import jax.numpy as jnp
from jax import lax
from jax.experimental import pallas as pl
from jax.experimental.pallas import tpu as pltpu
from jax.sharding import PartitionSpec as P

NLAT = 128
NLON = 128
CLASSES = 8
MESH = pl.DeviceIdType.MESH
HALO = 2 * NLON
PAD = 8

X_CHUNKS = ((14, 2), (0, 2), (2, 4), (6, 4), (10, 2), (12, 2))
X_RELAYED = (3, 4, 5)
Z_PIECES = ((2, 2), (4, 2), (0, 2), (6, 2))
Z_RELAYED = (0, 1)
ROW_BLOCK = 32


def lookup(codes, tab_ref, line):
    value = jnp.full(codes.shape, tab_ref[line, 0], jnp.float32)
    for cls in range(1, CLASSES):
        value = jnp.where(codes == cls, tab_ref[line, cls], value)
    return value


def weights_of(lat, wd_ref, ws_ref, tab_ref, dif_ref):
    inside = jnp.logical_and(lat >= 0, lat < NLAT)
    lat = jnp.clip(lat, 0, NLAT - 1)
    spot = pl.ds(pl.multiple_of(lat * NLON, NLON), NLON)
    direction = wd_ref[:, spot]
    speed = ws_ref[:, spot]
    u = lookup(speed, tab_ref, 0)
    v = lookup(speed, tab_ref, 1)
    e = jnp.where((direction & 1) == 0, 1.0, 0.0)
    n = jnp.where(direction < 2, 1.0, 0.0)
    k = dif_ref[lat]
    keep = jnp.where(inside, 1.0, 0.0)
    return [
        w * keep
        for w in (
            1.0 - u - v - 4.0 * k,
            u * e + k,
            u * (1.0 - e) + k,
            v * n + k,
            v * (1.0 - n) + k,
        )
    ]


def kernel(
    n_rows, n_cols, lat_r, lat_c,
    cov, wd_ref, ws_ref, tab_ref, dif_ref, out,
    X, B, CW, RW, G, RX, RZ, SH,
    lsem, xs, xr, zs, zr, rxs, rxr, rzs, rzr,
):
    r = lax.axis_index("row")
    c = lax.axis_index("col")
    left, right, up, down = c > 0, c < n_cols - 1, r > 0, r < n_rows - 1
    rows, cols = lat_r * NLON, lat_c * NLON

    def at(row, col):
        return {"row": row, "col": col}

    mid_r, mid_c = n_rows // 2, n_cols // 2
    q = lax.rem(c, mid_c)
    z_cross = jnp.logical_or(q < 2, q >= mid_c - 2)
    p = lax.rem(r, mid_r)
    x_cross = jnp.logical_or(p == 0, p == mid_r - 1)

    def z_role(row):
        return jnp.logical_and(z_cross, r == row)

    def x_role(col):
        return jnp.logical_and(x_cross, c == col)

    end_r, end_c = n_rows - 1, n_cols - 1
    peers = [(left, at(r, c - 1)), (right, at(r, c + 1)), (up, at(r - 1, c)), (down, at(r + 1, c))]
    for a, b in ((mid_r - 1, 0), (0, mid_r), (mid_r, end_r), (end_r, mid_r - 1)):
        peers += [(z_role(a), at(b, c)), (z_role(b), at(a, c))]
    for a, b in ((mid_c - 1, end_c), (end_c, mid_c), (mid_c, 0), (0, mid_c - 1)):
        peers += [(x_role(a), at(r, b)), (x_role(b), at(r, a))]

    own = [(rows - HALO, HALO), (0, HALO), (HALO, rows - 2 * HALO)]

    def own_copy(i):
        start, size = own[i]
        return pltpu.make_async_copy(
            cov.at[pl.ds(start, size), :], X.at[pl.ds(start, size), pl.ds(HALO, cols)], lsem.at[i]
        )

    barrier = pltpu.get_barrier_semaphore()
    for have, where in peers:
        @pl.when(have)
        def _():
            pl.semaphore_signal(barrier, inc=1, device_id=where, device_id_type=MESH)
    for i in range(3):
        own_copy(i).start()

    src_lon = lax.broadcasted_iota(jnp.int32, (2 * NLON, 2 * NLON), 0) & (NLON - 1)
    dst = lax.broadcasted_iota(jnp.int32, (2 * NLON, 2 * NLON), 1)
    step = jnp.where(dst < NLON, 1, NLON - 1)
    hit = ((src_lon + step) & (NLON - 1)) == (dst & (NLON - 1))
    SH[...] = jnp.where(hit, 1.0, 0.0).astype(jnp.bfloat16)

    def col_table(i, carry):
        for k, w in enumerate(weights_of(c * lat_c + i - 1, wd_ref, ws_ref, tab_ref, dif_ref)):
            for s in range(2):
                CW[s * 5 + k, i] = jnp.broadcast_to(w[s : s + 1], (8, NLON))
        return carry

    lax.fori_loop(0, lat_c + 2, col_table, 0, unroll=2)

    pl.semaphore_wait(barrier, sum(jnp.where(have, 1, 0) for have, _ in peers))

    def remote(src, dst, send, recv, where):
        return lambda: pltpu.make_async_remote_copy(
            src_ref=src, dst_ref=dst, send_sem=send, recv_sem=recv, device_id=where, device_id_type=MESH
        )

    def x_halo(i, side):
        lat, count = X_CHUNKS[i]
        return X.at[pl.ds(lat * NLON, count * NLON), pl.ds(0 if side == 0 else HALO + cols, HALO)]

    def x_stop(slot):
        return RX.at[slot, pl.ds(0, X_CHUNKS[X_RELAYED[slot]][1] * NLON)]

    def x_copies(i, side):
        lat, count = X_CHUNKS[i]
        src = cov.at[pl.ds(lat * NLON, count * NLON), pl.ds(cols - HALO if side == 0 else 0, HALO)]
        have, where = (right, at(r, c + 1)) if side == 0 else (left, at(r, c - 1))
        direct = remote(src, x_halo(i, side), xs.at[side, i], xr.at[side, i], where)
        if i not in X_RELAYED:
            return [(have, direct)]
        slot = X_RELAYED.index(i)
        source, relay = (mid_c - 1, end_c) if side == 0 else (mid_c, 0)
        by_relay = remote(src, x_stop(slot), xs.at[side, i], rxr.at[slot], at(r, relay))
        here = x_role(source)
        return [(jnp.logical_and(have, jnp.logical_not(here)), direct), (here, by_relay)]

    def x_forwards(slot):
        i = X_RELAYED[slot]
        return [
            (x_role(end_c), remote(x_stop(slot), x_halo(i, 0), rxs.at[slot], xr.at[0, i], at(r, mid_c))),
            (x_role(0), remote(x_stop(slot), x_halo(i, 1), rxs.at[slot], xr.at[1, i], at(r, mid_c - 1))),
        ]

    def z_halo(i, side):
        lat, count = Z_PIECES[i]
        return B.at[pl.ds(lat, count), pl.ds(0 if side == 0 else lat_r + 2, 2), pl.ds(PAD, NLON), :]

    def z_copies(i, side):
        lat, count = Z_PIECES[i]
        src = B.at[pl.ds(lat, count), pl.ds(lat_r if side == 0 else 2, 2), pl.ds(PAD, NLON), :]
        have, where = (down, at(r + 1, c)) if side == 0 else (up, at(r - 1, c))
        direct = remote(src, z_halo(i, side), zs.at[side, i], zr.at[side, i], where)
        if i not in Z_RELAYED:
            return [(have, direct)]
        slot = Z_RELAYED.index(i)
        source, relay = (mid_r - 1, 0) if side == 0 else (mid_r, end_r)
        by_relay = remote(src, RZ.at[slot], zs.at[side, i], rzr.at[slot], at(relay, c))
        here = z_role(source)
        return [(jnp.logical_and(have, jnp.logical_not(here)), direct), (here, by_relay)]

    def z_forwards(slot):
        i = Z_RELAYED[slot]
        return [
            (z_role(0), remote(RZ.at[slot], z_halo(i, 0), rzs.at[slot], zr.at[0, i], at(mid_r, c))),
            (z_role(end_r), remote(RZ.at[slot], z_halo(i, 1), rzs.at[slot], zr.at[1, i], at(mid_r - 1, c))),
        ]

    def start(copies):
        for have, copy in copies:
            @pl.when(have)
            def _():
                copy().start()

    def wait_sent(copies):
        for have, copy in copies:
            @pl.when(have)
            def _():
                copy().wait_send()

    def x_forward(slot):
        @pl.when(jnp.logical_or(x_role(0), x_role(end_c)))
        def _():
            x_copies(X_RELAYED[slot], 0)[1][1]().wait_recv()

        start(x_forwards(slot))

    def z_forward(slot):
        @pl.when(jnp.logical_or(z_role(0), z_role(end_r)))
        def _():
            z_copies(Z_RELAYED[slot], 0)[1][1]().wait_recv()

        start(z_forwards(slot))

    def z_start(i, side):
        start(z_copies(i, side))

    def z_wait(i):
        lat, count = Z_PIECES[i]
        for side, have in ((0, up), (1, down)):
            @pl.when(have)
            def _():
                z_copies(i, side)[0][1]().wait_recv()

            for a in (0, 1):
                y = a + (0 if side == 0 else lat_r + 2)
                for l in range(lat, lat + count):
                    B[l, y, pl.ds(0, PAD), :] = B[l, y, pl.ds(NLON, PAD), :]
                    B[l, y, pl.ds(PAD + NLON, PAD), :] = B[l, y, pl.ds(PAD, PAD), :]

    def x_wait(i):
        for side, have in ((0, left), (1, right)):
            @pl.when(have)
            def _():
                x_copies(i, side)[0][1]().wait_recv()

    def x_start(i, ways=slice(None)):
        for side in (0, 1):
            start(x_copies(i, side)[ways])

    DIRECT, BY_RELAY = slice(0, 1), slice(1, 2)

    x_start(0)
    x_start(1)
    for i in X_RELAYED:
        x_start(i, BY_RELAY)

    def stencil(f, west, east, south, north, w):
        return w[0] * f + w[1] * west + w[2] * east + w[3] * south + w[4] * north

    tiles = NLON // 8

    def column_operator(lat0, count, spans):
        def shifted(f, by_matrix):
            if not by_matrix:
                return pltpu.roll(f, 1, 2), pltpu.roll(f, NLON - 1, 2)
            flat = f.reshape(NLON, NLON)
            high = flat.astype(jnp.bfloat16)
            low = (flat - high.astype(jnp.float32)).astype(jnp.bfloat16)
            both = jnp.dot(
                jnp.concatenate([high, low], axis=1), SH[...], preferred_element_type=jnp.float32
            )
            return both[:, :NLON].reshape(f.shape), both[:, NLON:].reshape(f.shape)

        def lane_step(field, l, s):
            f = field[l]
            w = [CW[s * 5 + k, l + 1][None] for k in range(5)]
            return stencil(f, *shifted(f, s == 0), field[l - 1], field[l + 1], w)

        def body(i, carry):
            y = lat0 + i
            here = pl.ds(pl.multiple_of(y * NLON, NLON), NLON)
            for lo, hi in spans:
                f, g = {}, {}
                for l in range(lo - 2, hi + 2):
                    f[l] = X[here, pl.ds(HALO + l * NLON, NLON)].reshape(tiles, 8, NLON)
                    if l > lo - 1:
                        g[l - 1] = lane_step(f, l - 1, 0)
                    if l > lo + 1:
                        o = lane_step(g, l - 2, 1)
                        B[l - 2, y + 2, pl.ds(PAD, NLON), :] = o.reshape(NLON, NLON)
                        B[l - 2, y + 2, pl.ds(0, PAD), :] = o[tiles - 1]
                        B[l - 2, y + 2, pl.ds(PAD + NLON, PAD), :] = o[0]
            return carry

        lax.fori_loop(0, count, body, 0, unroll=2)

    def row_step(src, first, y, s, lat, store):
        for b in range(NLON // ROW_BLOCK):
            o = b * ROW_BLOCK
            w = [RW[s * 5 + k, lat + 1, pl.ds(o, ROW_BLOCK), :] for k in range(5)]
            for l in (0, 1):
                near = [src[first + l, y, pl.ds(PAD + o + d, ROW_BLOCK), :] for d in (0, -1, 1)]
                south = src[first + l, y - 1, pl.ds(PAD + o, ROW_BLOCK), :]
                north = src[first + l, y + 1, pl.ds(PAD + o, ROW_BLOCK), :]
                store(l, o, stencil(*near, south, north, w))

    def row_operator(lat0, count, pairs):
        first, n, stride = pairs

        def pair(j, carry):
            l0 = (first + j * stride) * 2
            span = [pl.ds(pl.multiple_of((l0 + l) * NLON, NLON), NLON) for l in (0, 1)]

            def one(i, inner):
                lat = lat0 - 1 + i

                def store(l, o, value):
                    G[l, i, pl.ds(PAD + o, ROW_BLOCK), :] = value
                    if o == 0:
                        G[l, i, pl.ds(PAD + NLON, PAD), :] = value[:PAD]
                    if o == NLON - ROW_BLOCK:
                        G[l, i, pl.ds(0, PAD), :] = value[ROW_BLOCK - PAD :]

                row_step(B, l0, lat + 2, 0, lat, store)
                return inner

            lax.fori_loop(0, count + 2, one, 0, unroll=2)

            def two(i, inner):
                lat = lat0 + i
                base = pl.multiple_of(lat * NLON, NLON)

                def store(l, o, value):
                    out[pl.ds(base + o, ROW_BLOCK), span[l]] = value

                row_step(G, 0, i + 1, 1, lat, store)
                return inner

            lax.fori_loop(0, count, two, 0, unroll=2)
            return carry

        lax.fori_loop(0, n, pair, 0)

    INNER, OUTER = (1, 2, 1), (0, 2, 3)
    inner, outer = ((2, lat_c - 2),), ((0, 2), (lat_c - 2, lat_c))

    own_copy(0).wait()
    column_operator(lat_r - 2, 2, inner)
    for i in (0, 1):
        z_start(i, 0)
    own_copy(1).wait()
    column_operator(0, 2, inner)
    for i in (0, 1):
        z_start(i, 1)

    def row_table(i, carry):
        lat = jnp.clip(r * lat_r + i - 1, 0, NLAT - 1)
        spot = pl.ds(pl.multiple_of(lat * NLON, NLON), NLON)
        direction, speed = wd_ref[:, spot], ws_ref[:, spot]
        u, v = lookup(speed, tab_ref, 0), lookup(speed, tab_ref, 1)
        u = jnp.where((direction & 1) == 0, u, -u)
        v = jnp.where(direction < 2, v, -v)
        k = dif_ref[lat]
        turned = jnp.concatenate([u, v, u, v], axis=0).T
        for s in range(2):
            su = jnp.broadcast_to(turned[:, s : s + 1], (NLON, NLON))
            sv = jnp.broadcast_to(turned[:, 2 + s : 3 + s], (NLON, NLON))
            RW[s * 5, i] = 1.0 - jnp.abs(su) - jnp.abs(sv) - 4.0 * k
            RW[s * 5 + 1, i] = jnp.maximum(su, 0.0) + k
            RW[s * 5 + 2, i] = jnp.maximum(-su, 0.0) + k
            RW[s * 5 + 3, i] = jnp.maximum(sv, 0.0) + k
            RW[s * 5 + 4, i] = jnp.maximum(-sv, 0.0) + k
        return carry

    lax.fori_loop(0, lat_r + 2, row_table, 0, unroll=2)

    @pl.when(jnp.logical_not(up))
    def _():
        RW[:, 0] = jnp.zeros((10, NLON, NLON), jnp.float32)

    @pl.when(jnp.logical_not(down))
    def _():
        RW[:, lat_r + 1] = jnp.zeros((10, NLON, NLON), jnp.float32)

    x_start(2)

    own_copy(2).wait()
    column_operator(10, 4, inner)

    @pl.when(jnp.logical_not(left))
    def _():
        X[:, pl.ds(0, HALO)] = jnp.zeros((rows, HALO), jnp.float32)

    @pl.when(jnp.logical_not(right))
    def _():
        X[:, pl.ds(HALO + cols, HALO)] = jnp.zeros((rows, HALO), jnp.float32)

    @pl.when(jnp.logical_not(up))
    def _():
        B[:, pl.ds(0, 2)] = jnp.zeros((lat_c, 2, NLON + 2 * PAD, NLON), jnp.float32)

    @pl.when(jnp.logical_not(down))
    def _():
        B[:, pl.ds(lat_r + 2, 2)] = jnp.zeros((lat_c, 2, NLON + 2 * PAD, NLON), jnp.float32)

    def edges(i):
        x_wait(i)
        column_operator(*X_CHUNKS[i], outer)

    x_forward(0)
    edges(0)
    for i in (2, 3):
        z_start(i, 0)
    edges(1)
    for i in (2, 3):
        z_start(i, 1)
    z_forward(0)
    x_start(3, DIRECT)

    column_operator(2, 4, inner)
    x_forward(1)
    edges(2)
    x_forward(2)
    x_start(4, DIRECT)
    x_start(5, DIRECT)
    z_forward(1)
    column_operator(6, 4, inner)
    row_operator(2, lat_r - 4, INNER)
    row_operator(2, 2, OUTER)
    edges(3)
    row_operator(4, 4, OUTER)
    edges(4)
    row_operator(8, 2, OUTER)
    edges(5)
    row_operator(10, 4, OUTER)
    z_wait(2)
    z_wait(3)
    row_operator(0, 2, OUTER)
    row_operator(lat_r - 2, 2, OUTER)
    z_wait(0)
    z_wait(1)
    row_operator(0, 2, INNER)
    row_operator(lat_r - 2, 2, INNER)

    for side in (0, 1):
        for i in range(len(X_CHUNKS)):
            wait_sent(x_copies(i, side))
        for i in range(len(Z_PIECES)):
            wait_sent(z_copies(i, side))
    for slot in range(len(X_RELAYED)):
        wait_sent(x_forwards(slot))
    for slot in range(len(Z_RELAYED)):
        wait_sent(z_forwards(slot))


def solution(mesh):
    n_rows, n_cols = mesh.shape["row"], mesh.shape["col"]
    lat_r, lat_c = NLAT // n_rows, NLAT // n_cols

    def local(cov, wd, ws, tab, dif):
        rows, cols = cov.shape
        vmem = pl.BlockSpec(memory_space=pltpu.VMEM)
        smem = pl.BlockSpec(memory_space=pltpu.SMEM)
        f32 = jnp.float32
        return pl.pallas_call(
            functools.partial(kernel, n_rows, n_cols, lat_r, lat_c),
            out_shape=pltpu.VMEM((rows, cols), f32),
            in_specs=[pl.BlockSpec(memory_space=pl.ANY), vmem, vmem, smem, smem],
            out_specs=vmem,
            scratch_shapes=[
                pltpu.VMEM((rows, cols + 2 * HALO), f32),
                pltpu.VMEM((lat_c, lat_r + 4, NLON + 2 * PAD, NLON), f32),
                pltpu.VMEM((10, lat_c + 2, 8, NLON), f32),
                pltpu.VMEM((10, lat_r + 2, NLON, NLON), f32),
                pltpu.VMEM((2, lat_r - 2, NLON + 2 * PAD, NLON), f32),
                pltpu.VMEM((len(X_RELAYED), 4 * NLON, HALO), f32),
                pltpu.VMEM((2, 2, 2, NLON, NLON), f32),
                pltpu.VMEM((2 * NLON, 2 * NLON), jnp.bfloat16),
                pltpu.SemaphoreType.DMA((3,)),
                pltpu.SemaphoreType.DMA((2, len(X_CHUNKS))),
                pltpu.SemaphoreType.DMA((2, len(X_CHUNKS))),
                pltpu.SemaphoreType.DMA((2, len(Z_PIECES))),
                pltpu.SemaphoreType.DMA((2, len(Z_PIECES))),
                pltpu.SemaphoreType.DMA((len(X_RELAYED),)),
                pltpu.SemaphoreType.DMA((len(X_RELAYED),)),
                pltpu.SemaphoreType.DMA((len(Z_RELAYED),)),
                pltpu.SemaphoreType.DMA((len(Z_RELAYED),)),
            ],
            compiler_params=pltpu.CompilerParams(
                collective_id=0, has_side_effects=True, vmem_limit_bytes=52 << 20
            ),
        )(cov, wd, ws, tab, dif)

    return jax.shard_map(
        local,
        mesh=mesh,
        in_specs=(P("row", "col"), P(), P(), P(), P()),
        out_specs=P("row", "col"),
        check_vma=False,
    )
```

```python
import functools

import jax
import jax.numpy as jnp
from jax import lax
from jax.experimental import pallas as pl
from jax.experimental.pallas import tpu as pltpu
from jax.sharding import PartitionSpec as P

NLAT = 128
NLON = 128
CLASSES = 8
MESH = pl.DeviceIdType.MESH
HALO = 2 * NLON
PAD = 8

X_CHUNKS = ((14, 2), (0, 2), (2, 4), (6, 4), (10, 2), (12, 2))
X_RELAYED = (3, 4, 5)
Z_PIECES = ((2, 2), (4, 2), (0, 2), (6, 2))
Z_RELAYED = (0, 1)
INNER, OUTER = (1, 2, 1), (0, 2, 3)
ROW_BLOCK = 32


def lookup(codes, tab_ref, line):
    value = jnp.full(codes.shape, tab_ref[line, 0], jnp.float32)
    for cls in range(1, CLASSES):
        value = jnp.where(codes == cls, tab_ref[line, cls], value)
    return value


def weights_of(lat, wd_ref, ws_ref, tab_ref, dif_ref):
    inside = jnp.logical_and(lat >= 0, lat < NLAT)
    lat = jnp.clip(lat, 0, NLAT - 1)
    spot = pl.ds(pl.multiple_of(lat * NLON, NLON), NLON)
    direction = wd_ref[:, spot]
    speed = ws_ref[:, spot]
    u = lookup(speed, tab_ref, 0)
    v = lookup(speed, tab_ref, 1)
    e = jnp.where((direction & 1) == 0, 1.0, 0.0)
    n = jnp.where(direction < 2, 1.0, 0.0)
    k = dif_ref[lat]
    keep = jnp.where(inside, 1.0, 0.0)
    return [
        w * keep
        for w in (
            1.0 - u - v - 4.0 * k,
            u * e + k,
            u * (1.0 - e) + k,
            v * n + k,
            v * (1.0 - n) + k,
        )
    ]


def stencil(f, west, east, south, north, w):
    return w[0] * f + w[1] * west + w[2] * east + w[3] * south + w[4] * north


def row_step(src, RW, first, y, s, lat, store):
    for b in range(NLON // ROW_BLOCK):
        o = b * ROW_BLOCK
        w = [RW[s * 5 + k, lat + 1, pl.ds(o, ROW_BLOCK), :] for k in range(5)]
        for l in (0, 1):
            near = [src[first + l, y, pl.ds(PAD + o + d, ROW_BLOCK), :] for d in (0, -1, 1)]
            south = src[first + l, y - 1, pl.ds(PAD + o, ROW_BLOCK), :]
            north = src[first + l, y + 1, pl.ds(PAD + o, ROW_BLOCK), :]
            store(l, o, stencil(*near, south, north, w))


def row_operator_into(out, B, RW, G, lat0, count, pairs):
    first, n, stride = pairs

    def pair(j, carry):
        l0 = (first + j * stride) * 2
        span = [pl.ds(pl.multiple_of((l0 + l) * NLON, NLON), NLON) for l in (0, 1)]

        def one(i, inner):
            lat = lat0 - 1 + i

            def store(l, o, value):
                G[l, i, pl.ds(PAD + o, ROW_BLOCK), :] = value
                if o == 0:
                    G[l, i, pl.ds(PAD + NLON, PAD), :] = value[:PAD]
                if o == NLON - ROW_BLOCK:
                    G[l, i, pl.ds(0, PAD), :] = value[ROW_BLOCK - PAD :]

            row_step(B, RW, l0, lat + 2, 0, lat, store)
            return inner

        lax.fori_loop(0, count + 2, one, 0, unroll=2)

        def two(i, inner):
            lat = lat0 + i
            base = pl.multiple_of(lat * NLON, NLON)

            def store(l, o, value):
                out[pl.ds(base + o, ROW_BLOCK), span[l]] = value

            row_step(G, RW, 0, i + 1, 1, lat, store)
            return inner

        lax.fori_loop(0, count, two, 0, unroll=2)
        return carry

    lax.fori_loop(0, n, pair, 0)


def kernel(
    n_rows, n_cols, lat_r, lat_c,
    cov, wd_hbm, ws_hbm, tab_hbm, dif_hbm, out, B, RW,
    X, CW, G, RX, RZ, SH, wd_ref, ws_ref, tab_ref, dif_ref,
    tsem, lsem, xs, xr, zs, zr, rxs, rxr, rzs, rzr,
):
    r = lax.axis_index("row")
    c = lax.axis_index("col")
    left, right, up, down = c > 0, c < n_cols - 1, r > 0, r < n_rows - 1
    rows, cols = lat_r * NLON, lat_c * NLON

    def at(row, col):
        return {"row": row, "col": col}

    mid_r, mid_c = n_rows // 2, n_cols // 2
    q = lax.rem(c, mid_c)
    z_cross = jnp.logical_or(q < 2, q >= mid_c - 2)
    p = lax.rem(r, mid_r)
    x_cross = jnp.logical_or(p == 0, p == mid_r - 1)

    def z_role(row):
        return jnp.logical_and(z_cross, r == row)

    def x_role(col):
        return jnp.logical_and(x_cross, c == col)

    end_r, end_c = n_rows - 1, n_cols - 1
    peers = [(left, at(r, c - 1)), (right, at(r, c + 1)), (up, at(r - 1, c)), (down, at(r + 1, c))]
    for a, b in ((mid_r - 1, 0), (0, mid_r), (mid_r, end_r), (end_r, mid_r - 1)):
        peers += [(z_role(a), at(b, c)), (z_role(b), at(a, c))]
    for a, b in ((mid_c - 1, end_c), (end_c, mid_c), (mid_c, 0), (0, mid_c - 1)):
        peers += [(x_role(a), at(r, b)), (x_role(b), at(r, a))]

    own = [(rows - HALO, HALO), (0, HALO), (HALO, rows - 2 * HALO)]

    def own_copy(i):
        start, size = own[i]
        return pltpu.make_async_copy(
            cov.at[pl.ds(start, size), :], X.at[pl.ds(start, size), pl.ds(HALO, cols)], lsem.at[i]
        )

    tables = [
        pltpu.make_async_copy(src, dst, tsem.at[i])
        for i, (src, dst) in enumerate(
            ((wd_hbm, wd_ref), (ws_hbm, ws_ref), (tab_hbm, tab_ref), (dif_hbm, dif_ref))
        )
    ]
    for copy in tables:
        copy.start()
    barrier = pltpu.get_barrier_semaphore()
    for have, where in peers:
        @pl.when(have)
        def _():
            pl.semaphore_signal(barrier, inc=1, device_id=where, device_id_type=MESH)
    for i in range(3):
        own_copy(i).start()

    src_lon = lax.broadcasted_iota(jnp.int32, (2 * NLON, 2 * NLON), 0) & (NLON - 1)
    dst = lax.broadcasted_iota(jnp.int32, (2 * NLON, 2 * NLON), 1)
    step = jnp.where(dst < NLON, 1, NLON - 1)
    hit = ((src_lon + step) & (NLON - 1)) == (dst & (NLON - 1))
    SH[...] = jnp.where(hit, 1.0, 0.0).astype(jnp.bfloat16)

    for copy in tables:
        copy.wait()

    def col_table(i, carry):
        for k, w in enumerate(weights_of(c * lat_c + i - 1, wd_ref, ws_ref, tab_ref, dif_ref)):
            for s in range(2):
                CW[s * 5 + k, i] = jnp.broadcast_to(w[s : s + 1], (8, NLON))
        return carry

    lax.fori_loop(0, lat_c + 2, col_table, 0, unroll=2)

    pl.semaphore_wait(barrier, sum(jnp.where(have, 1, 0) for have, _ in peers))

    def remote(src, dst, send, recv, where):
        return lambda: pltpu.make_async_remote_copy(
            src_ref=src, dst_ref=dst, send_sem=send, recv_sem=recv, device_id=where, device_id_type=MESH
        )

    def x_halo(i, side):
        lat, count = X_CHUNKS[i]
        return X.at[pl.ds(lat * NLON, count * NLON), pl.ds(0 if side == 0 else HALO + cols, HALO)]

    def x_stop(slot):
        return RX.at[slot, pl.ds(0, X_CHUNKS[X_RELAYED[slot]][1] * NLON)]

    def x_copies(i, side):
        lat, count = X_CHUNKS[i]
        src = cov.at[pl.ds(lat * NLON, count * NLON), pl.ds(cols - HALO if side == 0 else 0, HALO)]
        have, where = (right, at(r, c + 1)) if side == 0 else (left, at(r, c - 1))
        direct = remote(src, x_halo(i, side), xs.at[side, i], xr.at[side, i], where)
        if i not in X_RELAYED:
            return [(have, direct)]
        slot = X_RELAYED.index(i)
        source, relay = (mid_c - 1, end_c) if side == 0 else (mid_c, 0)
        by_relay = remote(src, x_stop(slot), xs.at[side, i], rxr.at[slot], at(r, relay))
        here = x_role(source)
        return [(jnp.logical_and(have, jnp.logical_not(here)), direct), (here, by_relay)]

    def x_forwards(slot):
        i = X_RELAYED[slot]
        return [
            (x_role(end_c), remote(x_stop(slot), x_halo(i, 0), rxs.at[slot], xr.at[0, i], at(r, mid_c))),
            (x_role(0), remote(x_stop(slot), x_halo(i, 1), rxs.at[slot], xr.at[1, i], at(r, mid_c - 1))),
        ]

    def z_halo(i, side):
        lat, count = Z_PIECES[i]
        return B.at[pl.ds(lat, count), pl.ds(0 if side == 0 else lat_r + 2, 2), pl.ds(PAD, NLON), :]

    def z_copies(i, side):
        lat, count = Z_PIECES[i]
        src = B.at[pl.ds(lat, count), pl.ds(lat_r if side == 0 else 2, 2), pl.ds(PAD, NLON), :]
        have, where = (down, at(r + 1, c)) if side == 0 else (up, at(r - 1, c))
        direct = remote(src, z_halo(i, side), zs.at[side, i], zr.at[side, i], where)
        if i not in Z_RELAYED:
            return [(have, direct)]
        slot = Z_RELAYED.index(i)
        source, relay = (mid_r - 1, 0) if side == 0 else (mid_r, end_r)
        by_relay = remote(src, RZ.at[slot], zs.at[side, i], rzr.at[slot], at(relay, c))
        here = z_role(source)
        return [(jnp.logical_and(have, jnp.logical_not(here)), direct), (here, by_relay)]

    def z_forwards(slot):
        i = Z_RELAYED[slot]
        return [
            (z_role(0), remote(RZ.at[slot], z_halo(i, 0), rzs.at[slot], zr.at[0, i], at(mid_r, c))),
            (z_role(end_r), remote(RZ.at[slot], z_halo(i, 1), rzs.at[slot], zr.at[1, i], at(mid_r - 1, c))),
        ]

    def start(copies):
        for have, copy in copies:
            @pl.when(have)
            def _():
                copy().start()

    def wait_sent(copies):
        for have, copy in copies:
            @pl.when(have)
            def _():
                copy().wait_send()

    def x_forward(slot):
        @pl.when(jnp.logical_or(x_role(0), x_role(end_c)))
        def _():
            x_copies(X_RELAYED[slot], 0)[1][1]().wait_recv()

        start(x_forwards(slot))

    def z_forward(slot):
        @pl.when(jnp.logical_or(z_role(0), z_role(end_r)))
        def _():
            z_copies(Z_RELAYED[slot], 0)[1][1]().wait_recv()

        start(z_forwards(slot))

    def z_start(i, side):
        start(z_copies(i, side))

    def z_wait(i):
        lat, count = Z_PIECES[i]
        for side, have in ((0, up), (1, down)):
            @pl.when(have)
            def _():
                z_copies(i, side)[0][1]().wait_recv()

            for a in (0, 1):
                y = a + (0 if side == 0 else lat_r + 2)
                for l in range(lat, lat + count):
                    B[l, y, pl.ds(0, PAD), :] = B[l, y, pl.ds(NLON, PAD), :]
                    B[l, y, pl.ds(PAD + NLON, PAD), :] = B[l, y, pl.ds(PAD, PAD), :]

    def x_wait(i):
        for side, have in ((0, left), (1, right)):
            @pl.when(have)
            def _():
                x_copies(i, side)[0][1]().wait_recv()

    def x_start(i, ways=slice(None)):
        for side in (0, 1):
            start(x_copies(i, side)[ways])

    DIRECT, BY_RELAY = slice(0, 1), slice(1, 2)

    x_start(0)
    x_start(1)
    for i in X_RELAYED:
        x_start(i, BY_RELAY)

    tiles = NLON // 8

    def column_operator(lat0, count, spans):
        def shifted(f, by_matrix):
            if not by_matrix:
                return pltpu.roll(f, 1, 2), pltpu.roll(f, NLON - 1, 2)
            flat = f.reshape(NLON, NLON)
            high = flat.astype(jnp.bfloat16)
            low = (flat - high.astype(jnp.float32)).astype(jnp.bfloat16)
            both = jnp.dot(
                jnp.concatenate([high, low], axis=1), SH[...], preferred_element_type=jnp.float32
            )
            return both[:, :NLON].reshape(f.shape), both[:, NLON:].reshape(f.shape)

        def lane_step(field, l, s):
            f = field[l]
            w = [CW[s * 5 + k, l + 1][None] for k in range(5)]
            return stencil(f, *shifted(f, s == 0), field[l - 1], field[l + 1], w)

        def body(i, carry):
            y = lat0 + i
            here = pl.ds(pl.multiple_of(y * NLON, NLON), NLON)
            for lo, hi in spans:
                f, g = {}, {}
                for l in range(lo - 2, hi + 2):
                    f[l] = X[here, pl.ds(HALO + l * NLON, NLON)].reshape(tiles, 8, NLON)
                    if l > lo - 1:
                        g[l - 1] = lane_step(f, l - 1, 0)
                    if l > lo + 1:
                        o = lane_step(g, l - 2, 1)
                        B[l - 2, y + 2, pl.ds(PAD, NLON), :] = o.reshape(NLON, NLON)
                        B[l - 2, y + 2, pl.ds(0, PAD), :] = o[tiles - 1]
                        B[l - 2, y + 2, pl.ds(PAD + NLON, PAD), :] = o[0]
            return carry

        lax.fori_loop(0, count, body, 0, unroll=2)

    def row_operator(lat0, count, pairs):
        row_operator_into(out, B, RW, G, lat0, count, pairs)

    inner, outer = ((2, lat_c - 2),), ((0, 2), (lat_c - 2, lat_c))

    own_copy(0).wait()
    column_operator(lat_r - 2, 2, inner)
    for i in (0, 1):
        z_start(i, 0)
    own_copy(1).wait()
    column_operator(0, 2, inner)
    for i in (0, 1):
        z_start(i, 1)

    def row_table(i, carry):
        lat = jnp.clip(r * lat_r + i - 1, 0, NLAT - 1)
        spot = pl.ds(pl.multiple_of(lat * NLON, NLON), NLON)
        direction, speed = wd_ref[:, spot], ws_ref[:, spot]
        u, v = lookup(speed, tab_ref, 0), lookup(speed, tab_ref, 1)
        u = jnp.where((direction & 1) == 0, u, -u)
        v = jnp.where(direction < 2, v, -v)
        k = dif_ref[lat]
        turned = jnp.concatenate([u, v, u, v], axis=0).T
        for s in range(2):
            su = jnp.broadcast_to(turned[:, s : s + 1], (NLON, NLON))
            sv = jnp.broadcast_to(turned[:, 2 + s : 3 + s], (NLON, NLON))
            RW[s * 5, i] = 1.0 - jnp.abs(su) - jnp.abs(sv) - 4.0 * k
            RW[s * 5 + 1, i] = jnp.maximum(su, 0.0) + k
            RW[s * 5 + 2, i] = jnp.maximum(-su, 0.0) + k
            RW[s * 5 + 3, i] = jnp.maximum(sv, 0.0) + k
            RW[s * 5 + 4, i] = jnp.maximum(-sv, 0.0) + k
        return carry

    lax.fori_loop(0, lat_r + 2, row_table, 0, unroll=2)

    @pl.when(jnp.logical_not(up))
    def _():
        RW[:, 0] = jnp.zeros((10, NLON, NLON), jnp.float32)

    @pl.when(jnp.logical_not(down))
    def _():
        RW[:, lat_r + 1] = jnp.zeros((10, NLON, NLON), jnp.float32)

    x_start(2)

    own_copy(2).wait()
    column_operator(10, 4, inner)

    @pl.when(jnp.logical_not(left))
    def _():
        X[:, pl.ds(0, HALO)] = jnp.zeros((rows, HALO), jnp.float32)

    @pl.when(jnp.logical_not(right))
    def _():
        X[:, pl.ds(HALO + cols, HALO)] = jnp.zeros((rows, HALO), jnp.float32)

    @pl.when(jnp.logical_not(up))
    def _():
        B[:, pl.ds(0, 2)] = jnp.zeros((lat_c, 2, NLON + 2 * PAD, NLON), jnp.float32)

    @pl.when(jnp.logical_not(down))
    def _():
        B[:, pl.ds(lat_r + 2, 2)] = jnp.zeros((lat_c, 2, NLON + 2 * PAD, NLON), jnp.float32)

    def edges(i):
        x_wait(i)
        column_operator(*X_CHUNKS[i], outer)

    x_forward(0)
    edges(0)
    for i in (2, 3):
        z_start(i, 0)
    edges(1)
    for i in (2, 3):
        z_start(i, 1)
    z_forward(0)
    x_start(3, DIRECT)

    column_operator(2, 4, inner)
    x_forward(1)
    edges(2)
    x_forward(2)
    x_start(4, DIRECT)
    x_start(5, DIRECT)
    z_forward(1)
    column_operator(6, 4, inner)
    row_operator(2, lat_r - 4, INNER)
    row_operator(2, 2, OUTER)
    edges(3)
    row_operator(4, 4, OUTER)
    edges(4)
    row_operator(8, 2, OUTER)
    edges(5)
    row_operator(10, 4, OUTER)
    for i in (2, 3, 0, 1):
        z_wait(i)

    for side in (0, 1):
        for i in range(len(X_CHUNKS)):
            wait_sent(x_copies(i, side))
        for i in range(len(Z_PIECES)):
            wait_sent(z_copies(i, side))
    for slot in range(len(X_RELAYED)):
        wait_sent(x_forwards(slot))
    for slot in range(len(Z_RELAYED)):
        wait_sent(z_forwards(slot))


def finish(lat_r, out, B, RW, hbm, T, G, sem):
    def send(src, i, lat, count, first, columns):
        area = (pl.ds(lat * NLON, count * NLON), pl.ds(first * NLON, columns * NLON))
        copy = pltpu.make_async_copy(src.at[area], hbm.at[area], sem.at[i])
        copy.start()
        return copy

    copies = [send(out, 0, 2, lat_r - 4, 0, 8)]
    row_operator_into(T, B, RW, G, 0, 2, OUTER)
    row_operator_into(T, B, RW, G, 0, 2, INNER)
    copies.append(send(T, 1, 0, 2, 0, 8))
    row_operator_into(T, B, RW, G, lat_r - 2, 2, OUTER)
    row_operator_into(T, B, RW, G, lat_r - 2, 2, INNER)
    copies.append(send(T, 2, lat_r - 2, 2, 0, 8))
    for copy in copies:
        copy.wait()


def solution(mesh):
    n_rows, n_cols = mesh.shape["row"], mesh.shape["col"]
    lat_r, lat_c = NLAT // n_rows, NLAT // n_cols

    def local(cov, wd, ws, tab, dif):
        rows, cols = cov.shape
        vmem = pl.BlockSpec(memory_space=pltpu.VMEM)
        f32 = jnp.float32
        out, B, RW = pl.pallas_call(
            functools.partial(kernel, n_rows, n_cols, lat_r, lat_c),
            out_shape=[
                pltpu.VMEM((rows, cols), f32),
                pltpu.VMEM((lat_c, lat_r + 4, NLON + 2 * PAD, NLON), f32),
                pltpu.VMEM((10, lat_r + 2, NLON, NLON), f32),
            ],
            in_specs=[pl.BlockSpec(memory_space=pltpu.MemorySpace.HBM)] * 5,
            out_specs=[vmem] * 3,
            scratch_shapes=[
                pltpu.VMEM((rows, cols + 2 * HALO), f32),
                pltpu.VMEM((10, lat_c + 2, 8, NLON), f32),
                pltpu.VMEM((2, lat_r - 2, NLON + 2 * PAD, NLON), f32),
                pltpu.VMEM((len(X_RELAYED), 4 * NLON, HALO), f32),
                pltpu.VMEM((2, 2, 2, NLON, NLON), f32),
                pltpu.VMEM((2 * NLON, 2 * NLON), jnp.bfloat16),
                pltpu.VMEM(wd.shape, jnp.int32),
                pltpu.VMEM(ws.shape, jnp.int32),
                pltpu.SMEM(tab.shape, f32),
                pltpu.SMEM(dif.shape, f32),
                pltpu.SemaphoreType.DMA((4,)),
                pltpu.SemaphoreType.DMA((3,)),
                pltpu.SemaphoreType.DMA((2, len(X_CHUNKS))),
                pltpu.SemaphoreType.DMA((2, len(X_CHUNKS))),
                pltpu.SemaphoreType.DMA((2, len(Z_PIECES))),
                pltpu.SemaphoreType.DMA((2, len(Z_PIECES))),
                pltpu.SemaphoreType.DMA((len(X_RELAYED),)),
                pltpu.SemaphoreType.DMA((len(X_RELAYED),)),
                pltpu.SemaphoreType.DMA((len(Z_RELAYED),)),
                pltpu.SemaphoreType.DMA((len(Z_RELAYED),)),
            ],
            compiler_params=pltpu.CompilerParams(
                collective_id=0, has_side_effects=True, vmem_limit_bytes=20 << 20
            ),
        )(*(pltpu.with_memory_space_constraint(a, pltpu.MemorySpace.HBM) for a in (cov, wd, ws, tab, dif)))
        return pl.pallas_call(
            functools.partial(finish, lat_r),
            out_shape=jax.ShapeDtypeStruct((rows, cols), f32),
            in_specs=[vmem] * 3,
            out_specs=pl.BlockSpec(memory_space=pl.ANY),
            scratch_shapes=[
                pltpu.VMEM((rows, cols), f32),
                pltpu.VMEM((2, 6, NLON + 2 * PAD, NLON), f32),
                pltpu.SemaphoreType.DMA((6,)),
            ],
            compiler_params=pltpu.CompilerParams(vmem_limit_bytes=14 << 20),
        )(out, B, RW)

    return jax.shard_map(
        local,
        mesh=mesh,
        in_specs=(P("row", "col"), P(), P(), P(), P()),
        out_specs=P("row", "col"),
        check_vma=False,
    )
```

```python
import functools

import jax
import jax.numpy as jnp
from jax import lax
from jax.experimental import pallas as pl
from jax.experimental.pallas import tpu as pltpu
from jax.sharding import PartitionSpec as P

NLAT = 128
NLON = 128
CLASSES = 8
MESH = pl.DeviceIdType.MESH
HALO = 2 * NLON
PAD = 8

X_CHUNKS = ((14, 2), (0, 2), (2, 4), (6, 4), (10, 2), (12, 2))
X_RELAYED = (3, 4, 5)
Z_PIECES = ((2, 2), (4, 2), (0, 2), (6, 2))
Z_RELAYED = (0, 1)
INNER, OUTER = (1, 2, 1), (0, 2, 3)
ROW_BLOCK = 32


def lookup(codes, tab_ref, line):
    value = jnp.full(codes.shape, tab_ref[line, 0], jnp.float32)
    for cls in range(1, CLASSES):
        value = jnp.where(codes == cls, tab_ref[line, cls], value)
    return value


def weights_of(lat, wd_ref, ws_ref, tab_ref, dif_ref):
    inside = jnp.logical_and(lat >= 0, lat < NLAT)
    lat = jnp.clip(lat, 0, NLAT - 1)
    spot = pl.ds(pl.multiple_of(lat * NLON, NLON), NLON)
    direction = wd_ref[:, spot]
    speed = ws_ref[:, spot]
    u = lookup(speed, tab_ref, 0)
    v = lookup(speed, tab_ref, 1)
    e = jnp.where((direction & 1) == 0, 1.0, 0.0)
    n = jnp.where(direction < 2, 1.0, 0.0)
    k = dif_ref[lat]
    keep = jnp.where(inside, 1.0, 0.0)
    return [
        w * keep
        for w in (
            1.0 - u - v - 4.0 * k,
            u * e + k,
            u * (1.0 - e) + k,
            v * n + k,
            v * (1.0 - n) + k,
        )
    ]


def stencil(f, west, east, south, north, w):
    return w[0] * f + w[1] * west + w[2] * east + w[3] * south + w[4] * north


def row_step(src, RW, first, y, s, lat, store):
    for b in range(NLON // ROW_BLOCK):
        o = b * ROW_BLOCK
        w = [RW[s * 5 + k, lat + 1, pl.ds(o, ROW_BLOCK), :] for k in range(5)]
        for l in (0, 1):
            near = [src[first + l, y, pl.ds(PAD + o + d, ROW_BLOCK), :] for d in (0, -1, 1)]
            south = src[first + l, y - 1, pl.ds(PAD + o, ROW_BLOCK), :]
            north = src[first + l, y + 1, pl.ds(PAD + o, ROW_BLOCK), :]
            store(l, o, stencil(*near, south, north, w))


def row_operator_into(out, B, RW, G, lat0, count, pairs):
    first, n, stride = pairs

    def pair(j, carry):
        l0 = (first + j * stride) * 2
        span = [pl.ds(pl.multiple_of((l0 + l) * NLON, NLON), NLON) for l in (0, 1)]

        def one(i, inner):
            lat = lat0 - 1 + i

            def store(l, o, value):
                G[l, i, pl.ds(PAD + o, ROW_BLOCK), :] = value
                if o == 0:
                    G[l, i, pl.ds(PAD + NLON, PAD), :] = value[:PAD]
                if o == NLON - ROW_BLOCK:
                    G[l, i, pl.ds(0, PAD), :] = value[ROW_BLOCK - PAD :]

            row_step(B, RW, l0, lat + 2, 0, lat, store)
            return inner

        lax.fori_loop(0, count + 2, one, 0, unroll=2)

        def two(i, inner):
            lat = lat0 + i
            base = pl.multiple_of(lat * NLON, NLON)

            def store(l, o, value):
                out[pl.ds(base + o, ROW_BLOCK), span[l]] = value

            row_step(G, RW, 0, i + 1, 1, lat, store)
            return inner

        lax.fori_loop(0, count, two, 0, unroll=2)
        return carry

    lax.fori_loop(0, n, pair, 0)


def kernel(
    n_rows, n_cols, lat_r, lat_c,
    cov, wd_hbm, ws_hbm, tab_hbm, dif_hbm, out, B, RW,
    X, CW, G, RX, RZ, SH, wd_ref, ws_ref, tab_ref, dif_ref,
    tsem, lsem, xs, xr, zs, zr, rxs, rxr, rzs, rzr,
):
    r = lax.axis_index("row")
    c = lax.axis_index("col")
    left, right, up, down = c > 0, c < n_cols - 1, r > 0, r < n_rows - 1
    rows, cols = lat_r * NLON, lat_c * NLON

    def at(row, col):
        return {"row": row, "col": col}

    mid_r, mid_c = n_rows // 2, n_cols // 2
    q = lax.rem(c, mid_c)
    z_cross = jnp.logical_or(q < 2, q >= mid_c - 2)
    p = lax.rem(r, mid_r)
    x_cross = jnp.logical_or(p == 0, p == mid_r - 1)

    def z_role(row):
        return jnp.logical_and(z_cross, r == row)

    def x_role(col):
        return jnp.logical_and(x_cross, c == col)

    end_r, end_c = n_rows - 1, n_cols - 1
    peers = [(left, at(r, c - 1)), (right, at(r, c + 1)), (up, at(r - 1, c)), (down, at(r + 1, c))]
    for a, b in ((mid_r - 1, 0), (0, mid_r), (mid_r, end_r), (end_r, mid_r - 1)):
        peers += [(z_role(a), at(b, c)), (z_role(b), at(a, c))]
    for a, b in ((mid_c - 1, end_c), (end_c, mid_c), (mid_c, 0), (0, mid_c - 1)):
        peers += [(x_role(a), at(r, b)), (x_role(b), at(r, a))]

    own = [(rows - HALO, HALO), (0, HALO), (HALO, rows - 2 * HALO)]

    def own_copy(i):
        start, size = own[i]
        return pltpu.make_async_copy(
            cov.at[pl.ds(start, size), :], X.at[pl.ds(start, size), pl.ds(HALO, cols)], lsem.at[i]
        )

    tables = [
        pltpu.make_async_copy(src, dst, tsem.at[i])
        for i, (src, dst) in enumerate(
            ((wd_hbm, wd_ref), (ws_hbm, ws_ref), (tab_hbm, tab_ref), (dif_hbm, dif_ref))
        )
    ]
    for copy in tables:
        copy.start()
    barrier = pltpu.get_barrier_semaphore()
    for have, where in peers:
        @pl.when(have)
        def _():
            pl.semaphore_signal(barrier, inc=1, device_id=where, device_id_type=MESH)
    for i in range(3):
        own_copy(i).start()

    src_lon = lax.broadcasted_iota(jnp.int32, (2 * NLON, 2 * NLON), 0) & (NLON - 1)
    dst = lax.broadcasted_iota(jnp.int32, (2 * NLON, 2 * NLON), 1)
    step = jnp.where(dst < NLON, 1, NLON - 1)
    hit = ((src_lon + step) & (NLON - 1)) == (dst & (NLON - 1))
    SH[...] = jnp.where(hit, 1.0, 0.0).astype(jnp.bfloat16)

    for copy in tables:
        copy.wait()

    def col_table(i, carry):
        for k, w in enumerate(weights_of(c * lat_c + i - 1, wd_ref, ws_ref, tab_ref, dif_ref)):
            for s in range(2):
                CW[s * 5 + k, i] = jnp.broadcast_to(w[s : s + 1], (8, NLON))
        return carry

    lax.fori_loop(0, lat_c + 2, col_table, 0, unroll=2)

    @pl.when(jnp.logical_not(left))
    def _():
        X[:, pl.ds(0, HALO)] = jnp.zeros((rows, HALO), jnp.float32)

    @pl.when(jnp.logical_not(right))
    def _():
        X[:, pl.ds(HALO + cols, HALO)] = jnp.zeros((rows, HALO), jnp.float32)

    @pl.when(jnp.logical_not(up))
    def _():
        B[:, pl.ds(0, 2)] = jnp.zeros((lat_c, 2, NLON + 2 * PAD, NLON), jnp.float32)

    @pl.when(jnp.logical_not(down))
    def _():
        B[:, pl.ds(lat_r + 2, 2)] = jnp.zeros((lat_c, 2, NLON + 2 * PAD, NLON), jnp.float32)

    pl.semaphore_wait(barrier, sum(jnp.where(have, 1, 0) for have, _ in peers))

    def remote(src, dst, send, recv, where):
        return lambda: pltpu.make_async_remote_copy(
            src_ref=src, dst_ref=dst, send_sem=send, recv_sem=recv, device_id=where, device_id_type=MESH
        )

    def x_halo(i, side):
        lat, count = X_CHUNKS[i]
        return X.at[pl.ds(lat * NLON, count * NLON), pl.ds(0 if side == 0 else HALO + cols, HALO)]

    def x_stop(slot):
        return RX.at[slot, pl.ds(0, X_CHUNKS[X_RELAYED[slot]][1] * NLON)]

    def x_copies(i, side):
        lat, count = X_CHUNKS[i]
        src = cov.at[pl.ds(lat * NLON, count * NLON), pl.ds(cols - HALO if side == 0 else 0, HALO)]
        have, where = (right, at(r, c + 1)) if side == 0 else (left, at(r, c - 1))
        direct = remote(src, x_halo(i, side), xs.at[side, i], xr.at[side, i], where)
        if i not in X_RELAYED:
            return [(have, direct)]
        slot = X_RELAYED.index(i)
        source, relay = (mid_c - 1, end_c) if side == 0 else (mid_c, 0)
        by_relay = remote(src, x_stop(slot), xs.at[side, i], rxr.at[slot], at(r, relay))
        here = x_role(source)
        return [(jnp.logical_and(have, jnp.logical_not(here)), direct), (here, by_relay)]

    def x_forwards(slot):
        i = X_RELAYED[slot]
        return [
            (x_role(end_c), remote(x_stop(slot), x_halo(i, 0), rxs.at[slot], xr.at[0, i], at(r, mid_c))),
            (x_role(0), remote(x_stop(slot), x_halo(i, 1), rxs.at[slot], xr.at[1, i], at(r, mid_c - 1))),
        ]

    def z_halo(i, side):
        lat, count = Z_PIECES[i]
        return B.at[pl.ds(lat, count), pl.ds(0 if side == 0 else lat_r + 2, 2), pl.ds(PAD, NLON), :]

    def z_copies(i, side):
        lat, count = Z_PIECES[i]
        src = B.at[pl.ds(lat, count), pl.ds(lat_r if side == 0 else 2, 2), pl.ds(PAD, NLON), :]
        have, where = (down, at(r + 1, c)) if side == 0 else (up, at(r - 1, c))
        direct = remote(src, z_halo(i, side), zs.at[side, i], zr.at[side, i], where)
        if i not in Z_RELAYED:
            return [(have, direct)]
        slot = Z_RELAYED.index(i)
        source, relay = (mid_r - 1, 0) if side == 0 else (mid_r, end_r)
        by_relay = remote(src, RZ.at[slot], zs.at[side, i], rzr.at[slot], at(relay, c))
        here = z_role(source)
        return [(jnp.logical_and(have, jnp.logical_not(here)), direct), (here, by_relay)]

    def z_forwards(slot):
        i = Z_RELAYED[slot]
        return [
            (z_role(0), remote(RZ.at[slot], z_halo(i, 0), rzs.at[slot], zr.at[0, i], at(mid_r, c))),
            (z_role(end_r), remote(RZ.at[slot], z_halo(i, 1), rzs.at[slot], zr.at[1, i], at(mid_r - 1, c))),
        ]

    def start(copies):
        for have, copy in copies:
            @pl.when(have)
            def _():
                copy().start()

    def wait_sent(copies):
        for have, copy in copies:
            @pl.when(have)
            def _():
                copy().wait_send()

    def x_forward(slot):
        @pl.when(jnp.logical_or(x_role(0), x_role(end_c)))
        def _():
            x_copies(X_RELAYED[slot], 0)[1][1]().wait_recv()

        start(x_forwards(slot))

    def z_forward(slot):
        @pl.when(jnp.logical_or(z_role(0), z_role(end_r)))
        def _():
            z_copies(Z_RELAYED[slot], 0)[1][1]().wait_recv()

        start(z_forwards(slot))

    def z_start(i, side):
        start(z_copies(i, side))

    def z_wait(i):
        lat, count = Z_PIECES[i]
        for side, have in ((0, up), (1, down)):
            @pl.when(have)
            def _():
                z_copies(i, side)[0][1]().wait_recv()

            for a in (0, 1):
                y = a + (0 if side == 0 else lat_r + 2)
                for l in range(lat, lat + count):
                    B[l, y, pl.ds(0, PAD), :] = B[l, y, pl.ds(NLON, PAD), :]
                    B[l, y, pl.ds(PAD + NLON, PAD), :] = B[l, y, pl.ds(PAD, PAD), :]

    def x_wait(i):
        for side, have in ((0, left), (1, right)):
            @pl.when(have)
            def _():
                x_copies(i, side)[0][1]().wait_recv()

    def x_start(i, ways=slice(None)):
        for side in (0, 1):
            start(x_copies(i, side)[ways])

    DIRECT, BY_RELAY = slice(0, 1), slice(1, 2)

    x_start(0)
    x_start(1)
    for i in X_RELAYED:
        x_start(i, BY_RELAY)

    tiles = NLON // 8

    def column_operator(lat0, count, spans):
        def shifted(f, by_matrix):
            if not by_matrix:
                return pltpu.roll(f, 1, 2), pltpu.roll(f, NLON - 1, 2)
            flat = f.reshape(NLON, NLON)
            high = flat.astype(jnp.bfloat16)
            low = (flat - high.astype(jnp.float32)).astype(jnp.bfloat16)
            both = jnp.dot(
                jnp.concatenate([high, low], axis=1), SH[...], preferred_element_type=jnp.float32
            )
            return both[:, :NLON].reshape(f.shape), both[:, NLON:].reshape(f.shape)

        def lane_step(field, l, s):
            f = field[l]
            w = [CW[s * 5 + k, l + 1][None] for k in range(5)]
            return stencil(f, *shifted(f, s == 0), field[l - 1], field[l + 1], w)

        def body(i, carry):
            y = lat0 + i
            here = pl.ds(pl.multiple_of(y * NLON, NLON), NLON)
            for lo, hi in spans:
                f, g = {}, {}
                for l in range(lo - 2, hi + 2):
                    f[l] = X[here, pl.ds(HALO + l * NLON, NLON)].reshape(tiles, 8, NLON)
                    if l > lo - 1:
                        g[l - 1] = lane_step(f, l - 1, 0)
                    if l > lo + 1:
                        o = lane_step(g, l - 2, 1)
                        B[l - 2, y + 2, pl.ds(PAD, NLON), :] = o.reshape(NLON, NLON)
                        B[l - 2, y + 2, pl.ds(0, PAD), :] = o[tiles - 1]
                        B[l - 2, y + 2, pl.ds(PAD + NLON, PAD), :] = o[0]
            return carry

        lax.fori_loop(0, count, body, 0, unroll=2)

    def row_operator(lat0, count, pairs):
        row_operator_into(out, B, RW, G, lat0, count, pairs)

    inner, outer = ((2, lat_c - 2),), ((0, 2), (lat_c - 2, lat_c))

    own_copy(0).wait()
    column_operator(lat_r - 2, 2, inner)
    for i in (0, 1):
        z_start(i, 0)
    own_copy(1).wait()
    column_operator(0, 2, inner)
    for i in (0, 1):
        z_start(i, 1)

    def row_table(i, carry):
        lat = jnp.clip(r * lat_r + i - 1, 0, NLAT - 1)
        spot = pl.ds(pl.multiple_of(lat * NLON, NLON), NLON)
        direction, speed = wd_ref[:, spot], ws_ref[:, spot]
        u, v = lookup(speed, tab_ref, 0), lookup(speed, tab_ref, 1)
        u = jnp.where((direction & 1) == 0, u, -u)
        v = jnp.where(direction < 2, v, -v)
        k = dif_ref[lat]
        turned = jnp.concatenate([u, v, u, v], axis=0).T
        for s in range(2):
            su = jnp.broadcast_to(turned[:, s : s + 1], (NLON, NLON))
            sv = jnp.broadcast_to(turned[:, 2 + s : 3 + s], (NLON, NLON))
            RW[s * 5, i] = 1.0 - jnp.abs(su) - jnp.abs(sv) - 4.0 * k
            RW[s * 5 + 1, i] = jnp.maximum(su, 0.0) + k
            RW[s * 5 + 2, i] = jnp.maximum(-su, 0.0) + k
            RW[s * 5 + 3, i] = jnp.maximum(sv, 0.0) + k
            RW[s * 5 + 4, i] = jnp.maximum(-sv, 0.0) + k
        return carry

    lax.fori_loop(0, lat_r + 2, row_table, 0, unroll=2)

    @pl.when(jnp.logical_not(up))
    def _():
        RW[:, 0] = jnp.zeros((10, NLON, NLON), jnp.float32)

    @pl.when(jnp.logical_not(down))
    def _():
        RW[:, lat_r + 1] = jnp.zeros((10, NLON, NLON), jnp.float32)

    x_start(2)

    own_copy(2).wait()
    column_operator(10, 4, inner)

    def edges(i):
        x_wait(i)
        column_operator(*X_CHUNKS[i], outer)

    x_forward(0)
    edges(0)
    for i in (2, 3):
        z_start(i, 0)
    edges(1)
    for i in (2, 3):
        z_start(i, 1)
    z_forward(0)
    x_start(3, DIRECT)

    column_operator(2, 4, inner)
    x_forward(1)
    edges(2)
    x_forward(2)
    x_start(4, DIRECT)
    x_start(5, DIRECT)
    z_forward(1)
    column_operator(6, 4, inner)
    row_operator(2, lat_r - 4, INNER)
    row_operator(2, 2, OUTER)
    edges(3)
    row_operator(4, 4, OUTER)
    edges(4)
    row_operator(8, 2, OUTER)
    edges(5)
    row_operator(10, 4, OUTER)
    for i in (2, 3, 0, 1):
        z_wait(i)

    for side in (0, 1):
        for i in range(len(X_CHUNKS)):
            wait_sent(x_copies(i, side))
        for i in range(len(Z_PIECES)):
            wait_sent(z_copies(i, side))
    for slot in range(len(X_RELAYED)):
        wait_sent(x_forwards(slot))
    for slot in range(len(Z_RELAYED)):
        wait_sent(z_forwards(slot))


def finish(lat_r, out, B, RW, hbm, T, G, sem):
    def send(src, i, lat, count, first, columns):
        area = (pl.ds(lat * NLON, count * NLON), pl.ds(first * NLON, columns * NLON))
        copy = pltpu.make_async_copy(src.at[area], hbm.at[area], sem.at[i])
        copy.start()
        return copy

    copies = [send(out, 0, 2, lat_r - 4, 0, 8)]
    row_operator_into(T, B, RW, G, 0, 2, OUTER)
    row_operator_into(T, B, RW, G, 0, 2, INNER)
    copies.append(send(T, 1, 0, 2, 0, 8))
    row_operator_into(T, B, RW, G, lat_r - 2, 2, OUTER)
    row_operator_into(T, B, RW, G, lat_r - 2, 2, INNER)
    copies.append(send(T, 2, lat_r - 2, 2, 0, 8))
    for copy in copies:
        copy.wait()


def solution(mesh):
    n_rows, n_cols = mesh.shape["row"], mesh.shape["col"]
    lat_r, lat_c = NLAT // n_rows, NLAT // n_cols

    def local(cov, wd, ws, tab, dif):
        rows, cols = cov.shape
        vmem = pl.BlockSpec(memory_space=pltpu.VMEM)
        f32 = jnp.float32
        out, B, RW = pl.pallas_call(
            functools.partial(kernel, n_rows, n_cols, lat_r, lat_c),
            out_shape=[
                pltpu.VMEM((rows, cols), f32),
                pltpu.VMEM((lat_c, lat_r + 4, NLON + 2 * PAD, NLON), f32),
                pltpu.VMEM((10, lat_r + 2, NLON, NLON), f32),
            ],
            in_specs=[pl.BlockSpec(memory_space=pltpu.MemorySpace.HBM)] * 5,
            out_specs=[vmem] * 3,
            scratch_shapes=[
                pltpu.VMEM((rows, cols + 2 * HALO), f32),
                pltpu.VMEM((10, lat_c + 2, 8, NLON), f32),
                pltpu.VMEM((2, lat_r - 2, NLON + 2 * PAD, NLON), f32),
                pltpu.VMEM((len(X_RELAYED), 4 * NLON, HALO), f32),
                pltpu.VMEM((2, 2, 2, NLON, NLON), f32),
                pltpu.VMEM((2 * NLON, 2 * NLON), jnp.bfloat16),
                pltpu.VMEM(wd.shape, jnp.int32),
                pltpu.VMEM(ws.shape, jnp.int32),
                pltpu.SMEM(tab.shape, f32),
                pltpu.SMEM(dif.shape, f32),
                pltpu.SemaphoreType.DMA((4,)),
                pltpu.SemaphoreType.DMA((3,)),
                pltpu.SemaphoreType.DMA((2, len(X_CHUNKS))),
                pltpu.SemaphoreType.DMA((2, len(X_CHUNKS))),
                pltpu.SemaphoreType.DMA((2, len(Z_PIECES))),
                pltpu.SemaphoreType.DMA((2, len(Z_PIECES))),
                pltpu.SemaphoreType.DMA((len(X_RELAYED),)),
                pltpu.SemaphoreType.DMA((len(X_RELAYED),)),
                pltpu.SemaphoreType.DMA((len(Z_RELAYED),)),
                pltpu.SemaphoreType.DMA((len(Z_RELAYED),)),
            ],
            compiler_params=pltpu.CompilerParams(
                collective_id=0, has_side_effects=True, vmem_limit_bytes=20 << 20
            ),
        )(*(pltpu.with_memory_space_constraint(a, pltpu.MemorySpace.HBM) for a in (cov, wd, ws, tab, dif)))
        return pl.pallas_call(
            functools.partial(finish, lat_r),
            out_shape=jax.ShapeDtypeStruct((rows, cols), f32),
            in_specs=[vmem] * 3,
            out_specs=pl.BlockSpec(memory_space=pl.ANY),
            scratch_shapes=[
                pltpu.VMEM((rows, cols), f32),
                pltpu.VMEM((2, 6, NLON + 2 * PAD, NLON), f32),
                pltpu.SemaphoreType.DMA((6,)),
            ],
            compiler_params=pltpu.CompilerParams(vmem_limit_bytes=14 << 20),
        )(out, B, RW)

    return jax.shard_map(
        local,
        mesh=mesh,
        in_specs=(P("row", "col"), P(), P(), P(), P()),
        out_specs=P("row", "col"),
        check_vma=False,
    )
```
